512 devices in a mesh: sec: 2 (over x_hi), wide: 128 (over z, x_lo, y), grp: 2 (over core).
Axes of the slice: x: 4 (x_hi: 2, x_lo: 2; x = x_hi * 2 + x_lo), y: 8, z: 8, core: 2. Of those that a mesh axis runs over, the one named last changes fastest.
Arguments:
- embeddings: bfloat16 [2, 131072, 1024], P('sec', ('wide', 'grp'))
- bin_ids: int32 [512], replicated, may hold values from 2 to 511, as said below
- positives: int32 [131072], P(('wide', 'grp')), may hold values from 0 to 131071, as said below
Outputs:
- grads: bfloat16 [2, 131072, 1024], P('sec', ('wide', 'grp'))
The draws below stay inside these ranges and needn't reach their ends.
Inputs may be any that keep to these rules, and one draw needn't show every extreme that they name: `bin_ids`: bin ids never fall from one block to the next; each id covers 1 to 3 consecutive blocks, the first id covers 3, and the last block's id is 511. positives maps the spectrum rows of each bin one to one onto the molecule rows of the same bin.
All inputs are finite; a program needn't handle non-finite values.
Results may differ from the reference program's by a relative error of at most 0.01.
Values may be sent and summed in bfloat16 or wider, within the bound.
A program may use at most 64 MiB of HBM per device.

```python
import jax
import jax.numpy as jnp
from jax import lax

E = 1024
BLOCK = 256
NB = 512
NROWS = 131072


def bin_layout(key):
    run_lengths = jax.random.randint(jax.random.fold_in(key, 11), (NB,), 1, 4)
    run_lengths = run_lengths.at[0].set(3)
    run_ends = jnp.cumsum(run_lengths)
    block_index = jnp.arange(NB, dtype=jnp.int32)
    run_number = jnp.sum((run_ends[None, :] <= block_index[:, None]).astype(jnp.int32), axis=1).astype(jnp.int32)
    last_number = jnp.sum((run_ends <= NB - 1).astype(jnp.int32)).astype(jnp.int32)
    return (run_number + (NB - 1) - last_number).astype(jnp.int32)


def draw_bin_ids(key, part):
    return bin_layout(key)


def draw_positives(key, part):
    row_bins = jnp.repeat(bin_layout(key), BLOCK)
    noise_draw = jax.random.randint(jax.random.fold_in(key, 12), (NROWS,), 0, NROWS)
    order_score = row_bins * NROWS + noise_draw
    return jnp.argsort(order_score, stable=True).astype(jnp.int32)


def draw_embeddings(key, part):
    half_width = E // 2
    row_bins = jnp.repeat(bin_layout(key), BLOCK)
    shared_base = jnp.clip(jax.random.normal(jax.random.fold_in(key, 3), (NB, half_width)), -4.5, 4.5)
    shared = 1.5 * shared_base
    noise_values = jnp.clip(jax.random.normal(jax.random.fold_in(key, 2), (2, NROWS, E)), -4.5, 4.5)
    second_half = 0.68 * noise_values[:, :, half_width:]
    common = jnp.take(shared, row_bins, axis=0)
    first_half = common[None] + 0.05 * noise_values[:, :, :half_width]
    return jnp.concatenate([first_half, second_half], axis=2).astype(jnp.bfloat16)


def setup_inputs(seed: int = 0) -> dict:
    streams_of = jax.random.split(jax.random.key(seed), 4)
    embeddings = draw_embeddings(jax.random.fold_in(streams_of[3], 71), 0)
    bin_ids = draw_bin_ids(jax.random.fold_in(streams_of[3], 71), 0)
    positives = draw_positives(jax.random.fold_in(streams_of[3], 71), 0)
    return {"embeddings": embeddings, "bin_ids": bin_ids, "positives": positives}


logit_scale = 0.125
reach_blocks = 2


def window_scores(queries, padded_keys, padded_bins, bin_ids, number):
    window_blocks = 2 * reach_blocks + 1
    query_rows = lax.dynamic_slice_in_dim(queries, number * BLOCK, BLOCK, 0)
    key_rows = lax.dynamic_slice_in_dim(padded_keys, number * BLOCK, window_blocks * BLOCK, 0)
    near_bins = lax.dynamic_slice_in_dim(padded_bins, number, window_blocks, 0)
    own_bin = lax.dynamic_slice_in_dim(bin_ids, number, 1, 0)
    allowed = jnp.repeat(near_bins == own_bin, BLOCK)
    scores = logit_scale * lax.dot_general(query_rows, key_rows, (((1,), (1,)), ((), ())), preferred_element_type=jnp.float32)
    return key_rows, jnp.where(allowed[None, :], scores, -jnp.inf)


def log_totals(queries, keys, bin_ids):
    margin = reach_blocks * BLOCK
    padded_keys = jnp.pad(keys, ((margin, margin), (0, 0)))
    padded_bins = jnp.pad(bin_ids, reach_blocks, constant_values=-1)

    def one_block(number):
        unused, scores = window_scores(queries, padded_keys, padded_bins, bin_ids, number)
        row_top = jnp.max(scores, axis=1, keepdims=True)
        return (jnp.log(jnp.sum(jnp.exp(scores - row_top), axis=1, keepdims=True)) + row_top)[:, 0]

    return lax.map(one_block, jnp.arange(NB, dtype=jnp.int32)).reshape(NROWS)


def spectra_grads(spectra, molecules, bin_ids, positives, row_totals, col_totals):
    margin = reach_blocks * BLOCK
    window_rows = (2 * reach_blocks + 1) * BLOCK
    padded_keys = jnp.pad(molecules, ((margin, margin), (0, 0)))
    padded_bins = jnp.pad(bin_ids, reach_blocks, constant_values=-1)
    padded_totals = jnp.pad(col_totals, margin)

    def one_block(number):
        key_rows, scores = window_scores(spectra, padded_keys, padded_bins, bin_ids, number)
        own_totals = lax.dynamic_slice_in_dim(row_totals, number * BLOCK, BLOCK, 0)
        near_totals = lax.dynamic_slice_in_dim(padded_totals, number * BLOCK, window_rows, 0)
        targets = lax.dynamic_slice_in_dim(positives, number * BLOCK, BLOCK, 0)
        columns = (number - reach_blocks) * BLOCK + jnp.arange(window_rows, dtype=jnp.int32)
        target_hits = (columns[None, :] == targets[:, None]).astype(jnp.float32)
        row_weights = (jnp.exp(scores - own_totals[:, None]) - 2.0 * target_hits).astype(jnp.bfloat16)
        col_weights = jnp.exp(scores - near_totals[None, :]).astype(jnp.bfloat16)
        summed = jnp.dot(row_weights, key_rows, preferred_element_type=jnp.float32) + jnp.dot(col_weights, key_rows, preferred_element_type=jnp.float32)
        return (logit_scale * summed).astype(jnp.bfloat16)

    return lax.map(one_block, jnp.arange(NB, dtype=jnp.int32)).reshape(NROWS, E)


def molecule_grads(spectra, molecules, bin_ids, positives, row_totals, col_totals):
    margin = reach_blocks * BLOCK
    window_rows = (2 * reach_blocks + 1) * BLOCK
    padded_keys = jnp.pad(spectra, ((margin, margin), (0, 0)))
    padded_bins = jnp.pad(bin_ids, reach_blocks, constant_values=-1)
    padded_totals = jnp.pad(row_totals, margin)
    padded_targets = jnp.pad(positives, margin, constant_values=-1)

    def one_block(number):
        key_rows, scores = window_scores(molecules, padded_keys, padded_bins, bin_ids, number)
        own_totals = lax.dynamic_slice_in_dim(col_totals, number * BLOCK, BLOCK, 0)
        near_totals = lax.dynamic_slice_in_dim(padded_totals, number * BLOCK, window_rows, 0)
        near_targets = lax.dynamic_slice_in_dim(padded_targets, number * BLOCK, window_rows, 0)
        own_index = number * BLOCK + jnp.arange(BLOCK, dtype=jnp.int32)
        target_hits = (near_targets[None, :] == own_index[:, None]).astype(jnp.float32)
        own_weights = jnp.exp(scores - own_totals[:, None]).astype(jnp.bfloat16)
        back_weights = (jnp.exp(scores - near_totals[None, :]) - 2.0 * target_hits).astype(jnp.bfloat16)
        summed = jnp.dot(own_weights, key_rows, preferred_element_type=jnp.float32) + jnp.dot(back_weights, key_rows, preferred_element_type=jnp.float32)
        return (logit_scale * summed).astype(jnp.bfloat16)

    return lax.map(one_block, jnp.arange(NB, dtype=jnp.int32)).reshape(NROWS, E)


def reference(embeddings, bin_ids, positives):
    spectra = embeddings[0]
    molecules = embeddings[1]
    row_totals = log_totals(spectra, molecules, bin_ids)
    col_totals = log_totals(molecules, spectra, bin_ids)
    grad_spectra = spectra_grads(spectra, molecules, bin_ids, positives, row_totals, col_totals)
    grad_molecules = molecule_grads(spectra, molecules, bin_ids, positives, row_totals, col_totals)
    return jnp.stack([grad_spectra, grad_molecules])
```

```python
import jax
import jax.numpy as jnp
from jax import lax
from jax.sharding import PartitionSpec as P

BLOCK = 256
logit_scale = 0.125
ROWS = ("wide", "grp")


def swapped(value, axis):
    pairs = [(source, source ^ 1) for source in range(lax.axis_size(axis))]
    return lax.ppermute(value, axis, pairs)


def neighbours(value, axis):
    count = lax.axis_size(axis)
    forward = [(i, i + 1) for i in range(count - 1)]
    backward = [(i + 1, i) for i in range(count - 1)]
    from_left = lax.ppermute(value, axis, forward)
    from_right = lax.ppermute(value, axis, backward)
    return from_left, from_right


def masked_lse(scores, allowed, axis):
    top = jnp.max(jnp.where(allowed, scores, -jnp.inf), axis=axis, keepdims=True)
    top = jnp.where(jnp.isfinite(top), top, 0.0)
    total = jnp.sum(jnp.where(allowed, jnp.exp(scores - top), 0.0), axis=axis, keepdims=True)
    return jnp.log(total) + top


def local(embeddings, bin_ids, positives):
    own = embeddings[0]
    row_count, features = own.shape
    blocks = row_count // BLOCK
    me = lax.axis_index(ROWS)
    first_row = me * row_count
    spectral = lax.axis_index("sec") == 0

    partner = swapped(own, "sec")
    own_left, own_right = neighbours(own, ROWS)
    pos_left, pos_right = neighbours(positives, ROWS)
    partner_left, partner_right = neighbours(partner, ROWS)

    own_win = jnp.concatenate([own_left, own, own_right], axis=0)
    partner_win = jnp.concatenate([partner_left, partner, partner_right], axis=0)
    pos_win = jnp.concatenate([pos_left, positives, pos_right], axis=0)
    win = 3 * row_count

    padded = jnp.pad(bin_ids, blocks, constant_values=-1)
    near_bins = lax.dynamic_slice_in_dim(padded, me * blocks, 3 * blocks, 0)
    row_bins = jnp.repeat(near_bins, BLOCK)
    own_bins = jnp.where(row_bins < 0, -1, row_bins)
    partner_bins = jnp.where(row_bins < 0, -2, row_bins)
    allowed = own_bins[:, None] == partner_bins[None, :]

    scores = logit_scale * lax.dot_general(
        own_win, partner_win, (((1,), (1,)), ((), ())), preferred_element_type=jnp.float32
    )
    partner_total = masked_lse(scores, allowed, 0)
    mine = slice(row_count, 2 * row_count)
    own_scores = scores[mine]
    own_allowed = allowed[mine]
    own_total = masked_lse(own_scores, own_allowed, 1)

    window_index = first_row - row_count + jnp.arange(win, dtype=jnp.int32)
    own_index = first_row + jnp.arange(row_count, dtype=jnp.int32)
    spectra_hits = window_index[None, :] == positives[:, None]
    molecule_hits = pos_win[None, :] == own_index[:, None]
    hits = jnp.where(spectral, spectra_hits, molecule_hits).astype(jnp.float32)

    weights = jnp.exp(own_scores - own_total) + jnp.exp(own_scores - partner_total)
    weights = jnp.where(own_allowed, weights, 0.0) - 2.0 * hits
    grad = logit_scale * jnp.dot(
        weights.astype(jnp.bfloat16), partner_win, preferred_element_type=jnp.float32
    )
    return grad.astype(jnp.bfloat16)[None]


def solution(mesh):
    in_specs = (P("sec", ROWS, None), P(), P(ROWS))
    out_specs = P("sec", ROWS, None)
    return jax.shard_map(local, mesh=mesh, in_specs=in_specs, out_specs=out_specs, check_vma=False)
```

```python
import functools

import jax
import jax.numpy as jnp
from jax import lax
from jax.experimental import pallas as pl
from jax.experimental.pallas import tpu as pltpu
from jax.sharding import PartitionSpec as P

BLOCK = 256
logit_scale = 0.125
ROWS = ("wide", "grp")


def swapped(value, axis):
    pairs = [(source, source ^ 1) for source in range(lax.axis_size(axis))]
    return lax.ppermute(value, axis, pairs)


def neighbours(value, axis):
    count = lax.axis_size(axis)
    forward = [(i, i + 1) for i in range(count - 1)]
    backward = [(i + 1, i) for i in range(count - 1)]
    from_left = lax.ppermute(value, axis, forward)
    from_right = lax.ppermute(value, axis, backward)
    return from_left, from_right


MESH_ID = pl.DeviceIdType.MESH
CHUNKS = 4


def exchange_kernel(groups, own_ref, zeros_ref, own_win, partner_win, local_sem,
                    sec_send, sec_recv, fwd_send, fwd_recv, halo_send, halo_recv):
    rows = own_ref.shape[0]
    piece = rows // CHUNKS
    sec = lax.axis_index("sec")
    wide = lax.axis_index("wide")
    grp = lax.axis_index("grp")
    count = lax.axis_size("wide") * groups
    me = wide * groups + grp
    has_left = me > 0
    has_right = me < count - 1
    partner_id = (1 - sec, wide, grp)
    left_id = (sec, (me - 1) // groups, (me - 1) % groups)
    right_id = (sec, (me + 1) // groups, (me + 1) % groups)

    barrier = pltpu.get_barrier_semaphore()
    pl.semaphore_signal(barrier, 1, device_id=partner_id, device_id_type=MESH_ID)

    @pl.when(has_left)
    def _():
        pl.semaphore_signal(barrier, 1, device_id=left_id, device_id_type=MESH_ID)

    @pl.when(has_right)
    def _():
        pl.semaphore_signal(barrier, 1, device_id=right_id, device_id_type=MESH_ID)

    peers = 1 + has_left.astype(jnp.int32) + has_right.astype(jnp.int32)
    pl.semaphore_wait(barrier, peers)

    def sec_copy(c):
        return pltpu.make_async_remote_copy(
            src_ref=own_ref.at[pl.ds(c * piece, piece)],
            dst_ref=partner_win.at[pl.ds(rows + c * piece, piece)],
            send_sem=sec_send.at[c], recv_sem=sec_recv.at[c],
            device_id=partner_id, device_id_type=MESH_ID)

    def halo_copy(d):
        return pltpu.make_async_remote_copy(
            src_ref=own_ref,
            dst_ref=own_win.at[pl.ds((1 - d) * 2 * rows, rows)],
            send_sem=halo_send.at[d], recv_sem=halo_recv.at[d],
            device_id=left_id if d == 0 else right_id, device_id_type=MESH_ID)

    def fwd_copy(d, c):
        return pltpu.make_async_remote_copy(
            src_ref=partner_win.at[pl.ds(rows + c * piece, piece)],
            dst_ref=partner_win.at[pl.ds((1 - d) * 2 * rows + c * piece, piece)],
            send_sem=fwd_send.at[d, c], recv_sem=fwd_recv.at[d, c],
            device_id=left_id if d == 0 else right_id, device_id_type=MESH_ID)

    for c in range(CHUNKS):
        sec_copy(c).start()
    sides = ((0, has_left), (1, has_right))
    for d, present in sides:
        @pl.when(present)
        def _():
            halo_copy(d).start()

    centre = pltpu.make_async_copy(own_ref, own_win.at[pl.ds(rows, rows)], local_sem.at[0])
    centre.start()

    for c in range(CHUNKS):
        sec_copy(c).wait_recv()
        for d, present in sides:
            @pl.when(present)
            def _():
                fwd_copy(d, c).start()

    for d, present in sides:
        @pl.when(present)
        def _():
            halo_copy(d).wait_send()
            for c in range(CHUNKS):
                fwd_copy(d, c).wait_send()

        arrived = has_right if d == 0 else has_left

        @pl.when(arrived)
        def _():
            halo_copy(d).wait_recv()
            for c in range(CHUNKS):
                fwd_copy(d, c).wait_recv()

    for c in range(CHUNKS):
        sec_copy(c).wait_send()
    centre.wait()

    for d, arrived in ((0, has_right), (1, has_left)):
        @pl.when(jnp.logical_not(arrived))
        def _():
            place = pl.ds((1 - d) * 2 * rows, rows)
            first = pltpu.make_async_copy(zeros_ref, own_win.at[place], local_sem.at[1])
            second = pltpu.make_async_copy(zeros_ref, partner_win.at[place], local_sem.at[2])
            first.start()
            second.start()
            first.wait()
            second.wait()


def exchange(own, groups):
    rows, features = own.shape
    window = jax.ShapeDtypeStruct((3 * rows, features), own.dtype)
    anywhere = pl.BlockSpec(memory_space=pl.ANY)
    return pl.pallas_call(
        functools.partial(exchange_kernel, groups),
        out_shape=(window, window),
        in_specs=[anywhere, anywhere],
        out_specs=(anywhere, anywhere),
        scratch_shapes=[
            pltpu.SemaphoreType.DMA((3,)),
            pltpu.SemaphoreType.DMA((CHUNKS,)),
            pltpu.SemaphoreType.DMA((CHUNKS,)),
            pltpu.SemaphoreType.DMA((2, CHUNKS)),
            pltpu.SemaphoreType.DMA((2, CHUNKS)),
            pltpu.SemaphoreType.DMA((2,)),
            pltpu.SemaphoreType.DMA((2,)),
        ],
        compiler_params=pltpu.CompilerParams(collective_id=0, has_side_effects=True),
    )(own, jnp.zeros_like(own))


def masked_lse(scores, allowed, axis):
    top = jnp.max(jnp.where(allowed, scores, -jnp.inf), axis=axis, keepdims=True)
    top = jnp.where(jnp.isfinite(top), top, 0.0)
    total = jnp.sum(jnp.where(allowed, jnp.exp(scores - top), 0.0), axis=axis, keepdims=True)
    return jnp.log(total) + top


def local(embeddings, bin_ids, positives):
    own = embeddings[0]
    row_count, features = own.shape
    blocks = row_count // BLOCK
    me = lax.axis_index(ROWS)
    first_row = me * row_count
    spectral = lax.axis_index("sec") == 0

    own_win, partner_win = exchange(own, lax.axis_size("grp"))
    pos_left, pos_right = neighbours(positives, ROWS)
    pos_win = jnp.concatenate([pos_left, positives, pos_right], axis=0)
    win = 3 * row_count

    padded = jnp.pad(bin_ids, blocks, constant_values=-1)
    near_bins = lax.dynamic_slice_in_dim(padded, me * blocks, 3 * blocks, 0)
    row_bins = jnp.repeat(near_bins, BLOCK)
    own_bins = jnp.where(row_bins < 0, -1, row_bins)
    partner_bins = jnp.where(row_bins < 0, -2, row_bins)
    allowed = own_bins[:, None] == partner_bins[None, :]

    scores = logit_scale * lax.dot_general(
        own_win, partner_win, (((1,), (1,)), ((), ())), preferred_element_type=jnp.float32
    )
    partner_total = masked_lse(scores, allowed, 0)
    mine = slice(row_count, 2 * row_count)
    own_scores = scores[mine]
    own_allowed = allowed[mine]
    own_total = masked_lse(own_scores, own_allowed, 1)

    window_index = first_row - row_count + jnp.arange(win, dtype=jnp.int32)
    own_index = first_row + jnp.arange(row_count, dtype=jnp.int32)
    spectra_hits = window_index[None, :] == positives[:, None]
    molecule_hits = pos_win[None, :] == own_index[:, None]
    hits = jnp.where(spectral, spectra_hits, molecule_hits).astype(jnp.float32)

    weights = jnp.exp(own_scores - own_total) + jnp.exp(own_scores - partner_total)
    weights = jnp.where(own_allowed, weights, 0.0) - 2.0 * hits
    grad = logit_scale * jnp.dot(
        weights.astype(jnp.bfloat16), partner_win, preferred_element_type=jnp.float32
    )
    return grad.astype(jnp.bfloat16)[None]


def solution(mesh):
    in_specs = (P("sec", ROWS, None), P(), P(ROWS))
    out_specs = P("sec", ROWS, None)
    return jax.shard_map(local, mesh=mesh, in_specs=in_specs, out_specs=out_specs, check_vma=False)
```

```python
import functools

import jax
import jax.numpy as jnp
from jax import lax
from jax.experimental import pallas as pl
from jax.experimental.pallas import tpu as pltpu
from jax.sharding import PartitionSpec as P

BLOCK = 256
logit_scale = 0.125
ROWS = ("wide", "grp")


def swapped(value, axis):
    pairs = [(source, source ^ 1) for source in range(lax.axis_size(axis))]
    return lax.ppermute(value, axis, pairs)


def neighbours(value, axis):
    count = lax.axis_size(axis)
    forward = [(i, i + 1) for i in range(count - 1)]
    backward = [(i + 1, i) for i in range(count - 1)]
    from_left = lax.ppermute(value, axis, forward)
    from_right = lax.ppermute(value, axis, backward)
    return from_left, from_right


MESH_ID = pl.DeviceIdType.MESH
CHUNKS = 4


def exchange_kernel(groups, own_ref, own_out, partner_out, own_win, partner_win, local_sem,
                    sec_send, sec_recv, fwd_send, fwd_recv, halo_send, halo_recv):
    rows = own_ref.shape[0]
    piece = rows // CHUNKS
    sec = lax.axis_index("sec")
    wide = lax.axis_index("wide")
    grp = lax.axis_index("grp")
    count = lax.axis_size("wide") * groups
    me = wide * groups + grp
    has_left = me > 0
    has_right = me < count - 1
    partner_id = (1 - sec, wide, grp)
    left_id = (sec, (me - 1) // groups, (me - 1) % groups)
    right_id = (sec, (me + 1) // groups, (me + 1) % groups)

    centre = pltpu.make_async_copy(own_ref, own_win.at[pl.ds(rows, rows)], local_sem.at[0])
    centre.start()

    for d, arrived in ((0, has_right), (1, has_left)):
        @pl.when(jnp.logical_not(arrived))
        def _():
            place = pl.ds((1 - d) * 2 * rows, rows)
            own_win[place, :] = jnp.zeros((rows, own_win.shape[1]), own_win.dtype)
            partner_win[place, :] = jnp.zeros((rows, own_win.shape[1]), own_win.dtype)

    barrier = pltpu.get_barrier_semaphore()
    pl.semaphore_signal(barrier, 1, device_id=partner_id, device_id_type=MESH_ID)

    @pl.when(has_left)
    def _():
        pl.semaphore_signal(barrier, 1, device_id=left_id, device_id_type=MESH_ID)

    @pl.when(has_right)
    def _():
        pl.semaphore_signal(barrier, 1, device_id=right_id, device_id_type=MESH_ID)

    peers = 1 + has_left.astype(jnp.int32) + has_right.astype(jnp.int32)
    pl.semaphore_wait(barrier, peers)

    def sec_copy(c):
        return pltpu.make_async_remote_copy(
            src_ref=own_ref.at[pl.ds(c * piece, piece)],
            dst_ref=partner_win.at[pl.ds(rows + c * piece, piece)],
            send_sem=sec_send.at[c], recv_sem=sec_recv.at[c],
            device_id=partner_id, device_id_type=MESH_ID)

    def halo_copy(d):
        return pltpu.make_async_remote_copy(
            src_ref=own_ref,
            dst_ref=own_win.at[pl.ds((1 - d) * 2 * rows, rows)],
            send_sem=halo_send.at[d], recv_sem=halo_recv.at[d],
            device_id=left_id if d == 0 else right_id, device_id_type=MESH_ID)

    def fwd_copy(d, c):
        return pltpu.make_async_remote_copy(
            src_ref=partner_win.at[pl.ds(rows + c * piece, piece)],
            dst_ref=partner_win.at[pl.ds((1 - d) * 2 * rows + c * piece, piece)],
            send_sem=fwd_send.at[d, c], recv_sem=fwd_recv.at[d, c],
            device_id=left_id if d == 0 else right_id, device_id_type=MESH_ID)

    for c in range(CHUNKS):
        sec_copy(c).start()
    sides = ((0, has_left), (1, has_right))
    for d, present in sides:
        @pl.when(present)
        def _():
            halo_copy(d).start()

    for c in range(CHUNKS):
        sec_copy(c).wait_recv()
        for d, present in sides:
            @pl.when(present)
            def _():
                fwd_copy(d, c).start()

    for d, present in sides:
        @pl.when(present)
        def _():
            halo_copy(d).wait_send()
            for c in range(CHUNKS):
                fwd_copy(d, c).wait_send()

        arrived = has_right if d == 0 else has_left

        @pl.when(arrived)
        def _():
            halo_copy(d).wait_recv()
            for c in range(CHUNKS):
                fwd_copy(d, c).wait_recv()

    for c in range(CHUNKS):
        sec_copy(c).wait_send()
    centre.wait()
    first = pltpu.make_async_copy(own_win, own_out, local_sem.at[1])
    second = pltpu.make_async_copy(partner_win, partner_out, local_sem.at[2])
    first.start()
    second.start()
    first.wait()
    second.wait()


def exchange(own, groups):
    rows, features = own.shape
    window = jax.ShapeDtypeStruct((3 * rows, features), own.dtype)
    anywhere = pl.BlockSpec(memory_space=pl.ANY)
    return pl.pallas_call(
        functools.partial(exchange_kernel, groups),
        out_shape=(window, window),
        in_specs=[anywhere],
        out_specs=(anywhere, anywhere),
        scratch_shapes=[
            pltpu.VMEM((3 * rows, features), own.dtype),
            pltpu.VMEM((3 * rows, features), own.dtype),
            pltpu.SemaphoreType.DMA((3,)),
            pltpu.SemaphoreType.DMA((CHUNKS,)),
            pltpu.SemaphoreType.DMA((CHUNKS,)),
            pltpu.SemaphoreType.DMA((2, CHUNKS)),
            pltpu.SemaphoreType.DMA((2, CHUNKS)),
            pltpu.SemaphoreType.DMA((2,)),
            pltpu.SemaphoreType.DMA((2,)),
        ],
        compiler_params=pltpu.CompilerParams(
            collective_id=0, has_side_effects=True, vmem_limit_bytes=32 * 1024 * 1024
        ),
    )(own)


def masked_lse(scores, allowed, axis):
    top = jnp.max(jnp.where(allowed, scores, -jnp.inf), axis=axis, keepdims=True)
    top = jnp.where(jnp.isfinite(top), top, 0.0)
    total = jnp.sum(jnp.where(allowed, jnp.exp(scores - top), 0.0), axis=axis, keepdims=True)
    return jnp.log(total) + top


def local(embeddings, bin_ids, positives):
    own = embeddings[0]
    row_count, features = own.shape
    blocks = row_count // BLOCK
    me = lax.axis_index(ROWS)
    first_row = me * row_count
    spectral = lax.axis_index("sec") == 0

    own_win, partner_win = exchange(own, lax.axis_size("grp"))
    pos_left, pos_right = neighbours(positives, ROWS)
    pos_win = jnp.concatenate([pos_left, positives, pos_right], axis=0)
    win = 3 * row_count

    padded = jnp.pad(bin_ids, blocks, constant_values=-1)
    near_bins = lax.dynamic_slice_in_dim(padded, me * blocks, 3 * blocks, 0)
    row_bins = jnp.repeat(near_bins, BLOCK)
    own_bins = jnp.where(row_bins < 0, -1, row_bins)
    partner_bins = jnp.where(row_bins < 0, -2, row_bins)
    allowed = own_bins[:, None] == partner_bins[None, :]

    scores = logit_scale * lax.dot_general(
        own_win, partner_win, (((1,), (1,)), ((), ())), preferred_element_type=jnp.float32
    )
    partner_total = masked_lse(scores, allowed, 0)
    mine = slice(row_count, 2 * row_count)
    own_scores = scores[mine]
    own_allowed = allowed[mine]
    own_total = masked_lse(own_scores, own_allowed, 1)

    window_index = first_row - row_count + jnp.arange(win, dtype=jnp.int32)
    own_index = first_row + jnp.arange(row_count, dtype=jnp.int32)
    spectra_hits = window_index[None, :] == positives[:, None]
    molecule_hits = pos_win[None, :] == own_index[:, None]
    hits = jnp.where(spectral, spectra_hits, molecule_hits).astype(jnp.float32)

    weights = jnp.exp(own_scores - own_total) + jnp.exp(own_scores - partner_total)
    weights = jnp.where(own_allowed, weights, 0.0) - 2.0 * hits
    grad = logit_scale * jnp.dot(
        weights.astype(jnp.bfloat16), partner_win, preferred_element_type=jnp.float32
    )
    return grad.astype(jnp.bfloat16)[None]


def solution(mesh):
    in_specs = (P("sec", ROWS, None), P(), P(ROWS))
    out_specs = P("sec", ROWS, None)
    return jax.shard_map(local, mesh=mesh, in_specs=in_specs, out_specs=out_specs, check_vma=False)
```

```python
import functools

import jax
import jax.numpy as jnp
from jax import lax
from jax.experimental import pallas as pl
from jax.experimental.pallas import tpu as pltpu
from jax.sharding import PartitionSpec as P

BLOCK = 256
logit_scale = 0.125
ROWS = ("wide", "grp")


def swapped(value, axis):
    pairs = [(source, source ^ 1) for source in range(lax.axis_size(axis))]
    return lax.ppermute(value, axis, pairs)


def neighbours(value, axis):
    count = lax.axis_size(axis)
    forward = [(i, i + 1) for i in range(count - 1)]
    backward = [(i + 1, i) for i in range(count - 1)]
    from_left = lax.ppermute(value, axis, forward)
    from_right = lax.ppermute(value, axis, backward)
    return from_left, from_right


MESH_ID = pl.DeviceIdType.MESH
PIECES = 2
Y_CHIPS = 8


def exchange_kernel(groups, own_ref, own_out, partner_out, own_win, partner_win, relay,
                    local_sem, hop_send, hop_recv, last_send, last_recv, fwd_send, fwd_recv,
                    halo_send, halo_recv):
    rows = own_ref.shape[0]
    half = rows // 2
    piece = half // PIECES
    sec = lax.axis_index("sec")
    wide = lax.axis_index("wide")
    grp = lax.axis_index("grp")
    count = lax.axis_size("wide") * groups
    me = wide * groups + grp
    has_left = me > 0
    has_right = me < count - 1
    left_id = (sec, (me - 1) // groups, (me - 1) % groups)
    right_id = (sec, (me + 1) // groups, (me + 1) % groups)
    ring = Y_CHIPS
    flipped = jnp.where((wide // ring) % 2 == 0, wide + ring, wide - ring)
    relay_id = ((sec, flipped, grp), (1 - sec, flipped, grp))

    centre = pltpu.make_async_copy(own_ref, own_win.at[pl.ds(rows, rows)], local_sem.at[0])
    centre.start()

    for d, arrived in ((0, has_right), (1, has_left)):
        @pl.when(jnp.logical_not(arrived))
        def _():
            place = pl.ds((1 - d) * 2 * rows, rows)
            own_win[place, :] = jnp.zeros((rows, own_win.shape[1]), own_win.dtype)
            partner_win[place, :] = jnp.zeros((rows, own_win.shape[1]), own_win.dtype)

    barrier = pltpu.get_barrier_semaphore()
    for k in range(2):
        pl.semaphore_signal(barrier, 1, device_id=relay_id[k], device_id_type=MESH_ID)

    @pl.when(has_left)
    def _():
        pl.semaphore_signal(barrier, 1, device_id=left_id, device_id_type=MESH_ID)

    @pl.when(has_right)
    def _():
        pl.semaphore_signal(barrier, 1, device_id=right_id, device_id_type=MESH_ID)

    peers = 2 + has_left.astype(jnp.int32) + has_right.astype(jnp.int32)
    pl.semaphore_wait(barrier, peers)

    def hop(k, p):
        return pltpu.make_async_remote_copy(
            src_ref=own_ref.at[pl.ds(k * half + p * piece, piece)],
            dst_ref=relay.at[k, pl.ds(p * piece, piece)],
            send_sem=hop_send.at[k, p], recv_sem=hop_recv.at[k, p],
            device_id=relay_id[k], device_id_type=MESH_ID)

    def last(k, p):
        return pltpu.make_async_remote_copy(
            src_ref=relay.at[k, pl.ds(p * piece, piece)],
            dst_ref=partner_win.at[pl.ds(rows + k * half + p * piece, piece)],
            send_sem=last_send.at[k, p], recv_sem=last_recv.at[k, p],
            device_id=relay_id[1 - k], device_id_type=MESH_ID)

    def halo_copy(d):
        return pltpu.make_async_remote_copy(
            src_ref=own_ref,
            dst_ref=own_win.at[pl.ds((1 - d) * 2 * rows, rows)],
            send_sem=halo_send.at[d], recv_sem=halo_recv.at[d],
            device_id=left_id if d == 0 else right_id, device_id_type=MESH_ID)

    def fwd_copy(d, q):
        return pltpu.make_async_remote_copy(
            src_ref=partner_win.at[pl.ds(rows + q * piece, piece)],
            dst_ref=partner_win.at[pl.ds((1 - d) * 2 * rows + q * piece, piece)],
            send_sem=fwd_send.at[d, q], recv_sem=fwd_recv.at[d, q],
            device_id=left_id if d == 0 else right_id, device_id_type=MESH_ID)

    for p in range(PIECES):
        for k in range(2):
            hop(k, p).start()
    sides = ((0, has_left), (1, has_right))
    for d, present in sides:
        @pl.when(present)
        def _():
            halo_copy(d).start()

    for p in range(PIECES):
        for k in range(2):
            hop(k, p).wait_recv()
            last(k, p).start()
    for p in range(PIECES):
        for k in range(2):
            last(k, p).wait_recv()
            q = k * PIECES + p
            for d, present in sides:
                @pl.when(present)
                def _():
                    fwd_copy(d, q).start()

    for d, present in sides:
        @pl.when(present)
        def _():
            halo_copy(d).wait_send()
            for q in range(2 * PIECES):
                fwd_copy(d, q).wait_send()

        arrived = has_right if d == 0 else has_left

        @pl.when(arrived)
        def _():
            halo_copy(d).wait_recv()
            for q in range(2 * PIECES):
                fwd_copy(d, q).wait_recv()

    for p in range(PIECES):
        for k in range(2):
            hop(k, p).wait_send()
            last(k, p).wait_send()
    centre.wait()
    first = pltpu.make_async_copy(own_win, own_out, local_sem.at[1])
    second = pltpu.make_async_copy(partner_win, partner_out, local_sem.at[2])
    first.start()
    second.start()
    first.wait()
    second.wait()


def exchange(own, groups):
    rows, features = own.shape
    window = jax.ShapeDtypeStruct((3 * rows, features), own.dtype)
    anywhere = pl.BlockSpec(memory_space=pl.ANY)
    return pl.pallas_call(
        functools.partial(exchange_kernel, groups),
        out_shape=(window, window),
        in_specs=[anywhere],
        out_specs=(anywhere, anywhere),
        scratch_shapes=[
            pltpu.VMEM((3 * rows, features), own.dtype),
            pltpu.VMEM((3 * rows, features), own.dtype),
            pltpu.VMEM((2, rows // 2, features), own.dtype),
            pltpu.SemaphoreType.DMA((3,)),
            pltpu.SemaphoreType.DMA((2, PIECES)),
            pltpu.SemaphoreType.DMA((2, PIECES)),
            pltpu.SemaphoreType.DMA((2, PIECES)),
            pltpu.SemaphoreType.DMA((2, PIECES)),
            pltpu.SemaphoreType.DMA((2, 2 * PIECES)),
            pltpu.SemaphoreType.DMA((2, 2 * PIECES)),
            pltpu.SemaphoreType.DMA((2,)),
            pltpu.SemaphoreType.DMA((2,)),
        ],
        compiler_params=pltpu.CompilerParams(
            collective_id=0, has_side_effects=True, vmem_limit_bytes=32 * 1024 * 1024
        ),
    )(own)


def masked_lse(scores, allowed, axis):
    top = jnp.max(jnp.where(allowed, scores, -jnp.inf), axis=axis, keepdims=True)
    top = jnp.where(jnp.isfinite(top), top, 0.0)
    total = jnp.sum(jnp.where(allowed, jnp.exp(scores - top), 0.0), axis=axis, keepdims=True)
    return jnp.log(total) + top


def local(embeddings, bin_ids, positives):
    own = embeddings[0]
    row_count, features = own.shape
    blocks = row_count // BLOCK
    me = lax.axis_index(ROWS)
    first_row = me * row_count
    spectral = lax.axis_index("sec") == 0

    own_win, partner_win = exchange(own, lax.axis_size("grp"))
    pos_left, pos_right = neighbours(positives, ROWS)
    pos_win = jnp.concatenate([pos_left, positives, pos_right], axis=0)
    win = 3 * row_count

    padded = jnp.pad(bin_ids, blocks, constant_values=-1)
    near_bins = lax.dynamic_slice_in_dim(padded, me * blocks, 3 * blocks, 0)
    row_bins = jnp.repeat(near_bins, BLOCK)
    own_bins = jnp.where(row_bins < 0, -1, row_bins)
    partner_bins = jnp.where(row_bins < 0, -2, row_bins)
    allowed = own_bins[:, None] == partner_bins[None, :]

    scores = logit_scale * lax.dot_general(
        own_win, partner_win, (((1,), (1,)), ((), ())), preferred_element_type=jnp.float32
    )
    partner_total = masked_lse(scores, allowed, 0)
    mine = slice(row_count, 2 * row_count)
    own_scores = scores[mine]
    own_allowed = allowed[mine]
    own_total = masked_lse(own_scores, own_allowed, 1)

    window_index = first_row - row_count + jnp.arange(win, dtype=jnp.int32)
    own_index = first_row + jnp.arange(row_count, dtype=jnp.int32)
    spectra_hits = window_index[None, :] == positives[:, None]
    molecule_hits = pos_win[None, :] == own_index[:, None]
    hits = jnp.where(spectral, spectra_hits, molecule_hits).astype(jnp.float32)

    weights = jnp.exp(own_scores - own_total) + jnp.exp(own_scores - partner_total)
    weights = jnp.where(own_allowed, weights, 0.0) - 2.0 * hits
    grad = logit_scale * jnp.dot(
        weights.astype(jnp.bfloat16), partner_win, preferred_element_type=jnp.float32
    )
    return grad.astype(jnp.bfloat16)[None]


def solution(mesh):
    in_specs = (P("sec", ROWS, None), P(), P(ROWS))
    out_specs = P("sec", ROWS, None)
    return jax.shard_map(local, mesh=mesh, in_specs=in_specs, out_specs=out_specs, check_vma=False)
```

```python
import functools

import jax
import jax.numpy as jnp
from jax import lax
from jax.experimental import pallas as pl
from jax.experimental.pallas import tpu as pltpu
from jax.sharding import PartitionSpec as P

BLOCK = 256
logit_scale = 0.125
ROWS = ("wide", "grp")


def swapped(value, axis):
    pairs = [(source, source ^ 1) for source in range(lax.axis_size(axis))]
    return lax.ppermute(value, axis, pairs)


def neighbours(value, axis):
    count = lax.axis_size(axis)
    forward = [(i, i + 1) for i in range(count - 1)]
    backward = [(i + 1, i) for i in range(count - 1)]
    from_left = lax.ppermute(value, axis, forward)
    from_right = lax.ppermute(value, axis, backward)
    return from_left, from_right


MESH_ID = pl.DeviceIdType.MESH
PIECES = 2
Y_CHIPS = 8


def exchange_kernel(groups, own_ref, pos_ref, own_out, partner_out, pos_out, own_win,
                    partner_win, pos_win, relay, local_sem, hop_send, hop_recv, last_send,
                    last_recv, fwd_send, fwd_recv, halo_send, halo_recv):
    rows = own_ref.shape[0]
    half = rows // 2
    piece = half // PIECES
    sec = lax.axis_index("sec")
    wide = lax.axis_index("wide")
    grp = lax.axis_index("grp")
    count = lax.axis_size("wide") * groups
    me = wide * groups + grp
    has_left = me > 0
    has_right = me < count - 1
    left_id = (sec, (me - 1) // groups, (me - 1) % groups)
    right_id = (sec, (me + 1) // groups, (me + 1) % groups)
    ring = Y_CHIPS
    flipped = jnp.where((wide // ring) % 2 == 0, wide + ring, wide - ring)
    relay_id = ((sec, flipped, grp), (1 - sec, flipped, grp))

    centre = pltpu.make_async_copy(own_ref, own_win.at[pl.ds(rows, rows)], local_sem.at[0])
    centre.start()
    lines = pos_ref.shape[0]
    pos_centre = pltpu.make_async_copy(pos_ref, pos_win.at[pl.ds(lines, lines)], local_sem.at[3])
    pos_centre.start()

    for d, arrived in ((0, has_right), (1, has_left)):
        @pl.when(jnp.logical_not(arrived))
        def _():
            place = pl.ds((1 - d) * 2 * rows, rows)
            own_win[place, :] = jnp.zeros((rows, own_win.shape[1]), own_win.dtype)
            partner_win[place, :] = jnp.zeros((rows, own_win.shape[1]), own_win.dtype)
            pos_win[pl.ds((1 - d) * 2 * lines, lines), :] = jnp.zeros(pos_ref.shape, jnp.int32)

    barrier = pltpu.get_barrier_semaphore()
    for k in range(2):
        pl.semaphore_signal(barrier, 1, device_id=relay_id[k], device_id_type=MESH_ID)

    @pl.when(has_left)
    def _():
        pl.semaphore_signal(barrier, 1, device_id=left_id, device_id_type=MESH_ID)

    @pl.when(has_right)
    def _():
        pl.semaphore_signal(barrier, 1, device_id=right_id, device_id_type=MESH_ID)

    peers = 2 + has_left.astype(jnp.int32) + has_right.astype(jnp.int32)
    pl.semaphore_wait(barrier, peers)

    def hop(k, p):
        return pltpu.make_async_remote_copy(
            src_ref=own_ref.at[pl.ds(k * half + p * piece, piece)],
            dst_ref=relay.at[k, pl.ds(p * piece, piece)],
            send_sem=hop_send.at[k, p], recv_sem=hop_recv.at[k, p],
            device_id=relay_id[k], device_id_type=MESH_ID)

    def last(k, p):
        return pltpu.make_async_remote_copy(
            src_ref=relay.at[k, pl.ds(p * piece, piece)],
            dst_ref=partner_win.at[pl.ds(rows + k * half + p * piece, piece)],
            send_sem=last_send.at[k, p], recv_sem=last_recv.at[k, p],
            device_id=relay_id[1 - k], device_id_type=MESH_ID)

    def halo_copy(d):
        return pltpu.make_async_remote_copy(
            src_ref=own_ref,
            dst_ref=own_win.at[pl.ds((1 - d) * 2 * rows, rows)],
            send_sem=halo_send.at[d], recv_sem=halo_recv.at[d],
            device_id=left_id if d == 0 else right_id, device_id_type=MESH_ID)

    def pos_copy(d):
        return pltpu.make_async_remote_copy(
            src_ref=pos_ref,
            dst_ref=pos_win.at[pl.ds((1 - d) * 2 * lines, lines)],
            send_sem=halo_send.at[2 + d], recv_sem=halo_recv.at[2 + d],
            device_id=left_id if d == 0 else right_id, device_id_type=MESH_ID)

    def fwd_copy(d, q):
        return pltpu.make_async_remote_copy(
            src_ref=partner_win.at[pl.ds(rows + q * piece, piece)],
            dst_ref=partner_win.at[pl.ds((1 - d) * 2 * rows + q * piece, piece)],
            send_sem=fwd_send.at[d, q], recv_sem=fwd_recv.at[d, q],
            device_id=left_id if d == 0 else right_id, device_id_type=MESH_ID)

    for p in range(PIECES):
        for k in range(2):
            hop(k, p).start()
    sides = ((0, has_left), (1, has_right))
    for d, present in sides:
        @pl.when(present)
        def _():
            pos_copy(d).start()
            halo_copy(d).start()

    for p in range(PIECES):
        for k in range(2):
            hop(k, p).wait_recv()
            last(k, p).start()
    for p in range(PIECES):
        for k in range(2):
            last(k, p).wait_recv()
            q = k * PIECES + p
            for d, present in sides:
                @pl.when(present)
                def _():
                    fwd_copy(d, q).start()

    for d, present in sides:
        @pl.when(present)
        def _():
            pos_copy(d).wait_send()
            halo_copy(d).wait_send()
            for q in range(2 * PIECES):
                fwd_copy(d, q).wait_send()

        arrived = has_right if d == 0 else has_left

        @pl.when(arrived)
        def _():
            pos_copy(d).wait_recv()
            halo_copy(d).wait_recv()
            for q in range(2 * PIECES):
                fwd_copy(d, q).wait_recv()

    for p in range(PIECES):
        for k in range(2):
            hop(k, p).wait_send()
            last(k, p).wait_send()
    centre.wait()
    pos_centre.wait()
    outs = ((own_win, own_out), (partner_win, partner_out), (pos_win, pos_out))
    copies = [pltpu.make_async_copy(a, b, local_sem.at[1 + n]) for n, (a, b) in enumerate(outs)]
    for copy in copies:
        copy.start()
    for copy in copies:
        copy.wait()


def exchange(own, positives, groups):
    rows, features = own.shape
    lanes = 128
    lined = positives.reshape(rows // lanes, lanes)
    window = jax.ShapeDtypeStruct((3 * rows, features), own.dtype)
    pos_window = jax.ShapeDtypeStruct((3 * rows // lanes, lanes), jnp.int32)
    anywhere = pl.BlockSpec(memory_space=pl.ANY)
    own_win, partner_win, pos_win = pl.pallas_call(
        functools.partial(exchange_kernel, groups),
        out_shape=(window, window, pos_window),
        in_specs=[anywhere, anywhere],
        out_specs=(anywhere, anywhere, anywhere),
        scratch_shapes=[
            pltpu.VMEM((3 * rows, features), own.dtype),
            pltpu.VMEM((3 * rows, features), own.dtype),
            pltpu.VMEM((3 * rows // lanes, lanes), jnp.int32),
            pltpu.VMEM((2, rows // 2, features), own.dtype),
            pltpu.SemaphoreType.DMA((4,)),
            pltpu.SemaphoreType.DMA((2, PIECES)),
            pltpu.SemaphoreType.DMA((2, PIECES)),
            pltpu.SemaphoreType.DMA((2, PIECES)),
            pltpu.SemaphoreType.DMA((2, PIECES)),
            pltpu.SemaphoreType.DMA((2, 2 * PIECES)),
            pltpu.SemaphoreType.DMA((2, 2 * PIECES)),
            pltpu.SemaphoreType.DMA((4,)),
            pltpu.SemaphoreType.DMA((4,)),
        ],
        compiler_params=pltpu.CompilerParams(
            collective_id=0, has_side_effects=True, vmem_limit_bytes=32 * 1024 * 1024
        ),
    )(own, lined)
    return own_win, partner_win, pos_win.reshape(3 * rows)


def masked_lse(scores, allowed, axis):
    top = jnp.max(jnp.where(allowed, scores, -jnp.inf), axis=axis, keepdims=True)
    top = jnp.where(jnp.isfinite(top), top, 0.0)
    total = jnp.sum(jnp.where(allowed, jnp.exp(scores - top), 0.0), axis=axis, keepdims=True)
    return jnp.log(total) + top


def local(embeddings, bin_ids, positives):
    own = embeddings[0]
    row_count, features = own.shape
    blocks = row_count // BLOCK
    me = lax.axis_index(ROWS)
    first_row = me * row_count
    spectral = lax.axis_index("sec") == 0

    own_win, partner_win, pos_win = exchange(own, positives, lax.axis_size("grp"))
    win = 3 * row_count

    padded = jnp.pad(bin_ids, blocks, constant_values=-1)
    near_bins = lax.dynamic_slice_in_dim(padded, me * blocks, 3 * blocks, 0)
    row_bins = jnp.repeat(near_bins, BLOCK)
    own_bins = jnp.where(row_bins < 0, -1, row_bins)
    partner_bins = jnp.where(row_bins < 0, -2, row_bins)
    allowed = own_bins[:, None] == partner_bins[None, :]

    scores = logit_scale * lax.dot_general(
        own_win, partner_win, (((1,), (1,)), ((), ())), preferred_element_type=jnp.float32
    )
    partner_total = masked_lse(scores, allowed, 0)
    mine = slice(row_count, 2 * row_count)
    own_scores = scores[mine]
    own_allowed = allowed[mine]
    own_total = masked_lse(own_scores, own_allowed, 1)

    window_index = first_row - row_count + jnp.arange(win, dtype=jnp.int32)
    own_index = first_row + jnp.arange(row_count, dtype=jnp.int32)
    spectra_hits = window_index[None, :] == positives[:, None]
    molecule_hits = pos_win[None, :] == own_index[:, None]
    hits = jnp.where(spectral, spectra_hits, molecule_hits) & own_allowed
    hits = hits.astype(jnp.float32)

    weights = jnp.exp(own_scores - own_total) + jnp.exp(own_scores - partner_total)
    weights = jnp.where(own_allowed, weights, 0.0) - 2.0 * hits
    grad = logit_scale * jnp.dot(
        weights.astype(jnp.bfloat16), partner_win, preferred_element_type=jnp.float32
    )
    return grad.astype(jnp.bfloat16)[None]


def solution(mesh):
    in_specs = (P("sec", ROWS, None), P(), P(ROWS))
    out_specs = P("sec", ROWS, None)
    return jax.shard_map(local, mesh=mesh, in_specs=in_specs, out_specs=out_specs, check_vma=False)
```

```python
import functools

import jax
import jax.numpy as jnp
from jax import lax
from jax.experimental import pallas as pl
from jax.experimental.pallas import tpu as pltpu
from jax.sharding import PartitionSpec as P

BLOCK = 256
logit_scale = 0.125
ROWS = ("wide", "grp")


MESH_ID = pl.DeviceIdType.MESH
PIECES = 2
Y_CHIPS = 8


def place_of(groups):
    sec = lax.axis_index("sec")
    wide = lax.axis_index("wide")
    grp = lax.axis_index("grp")
    count = lax.axis_size("wide") * groups
    me = wide * groups + grp
    left_id = (sec, (me - 1) // groups, (me - 1) % groups)
    right_id = (sec, (me + 1) // groups, (me + 1) % groups)
    return sec, wide, grp, me > 0, me < count - 1, left_id, right_id


def greet(peers_always, sides):
    barrier = pltpu.get_barrier_semaphore()
    for peer in peers_always:
        pl.semaphore_signal(barrier, 1, device_id=peer, device_id_type=MESH_ID)
    peers = len(peers_always)
    for present, peer in sides:
        @pl.when(present)
        def _():
            pl.semaphore_signal(barrier, 1, device_id=peer, device_id_type=MESH_ID)

        peers = peers + present.astype(jnp.int32)
    pl.semaphore_wait(barrier, peers)


def exchange_kernel(groups, own_ref, pos_ref, partner_out, pos_out, partner_win, pos_win,
                    relay, local_sem, hop_send, hop_recv, last_send, last_recv, fwd_send,
                    fwd_recv, halo_send, halo_recv):
    rows = own_ref.shape[0]
    half = rows // 2
    piece = half // PIECES
    lines = pos_ref.shape[0]
    sec, wide, grp, has_left, has_right, left_id, right_id = place_of(groups)
    ring = Y_CHIPS
    flipped = jnp.where((wide // ring) % 2 == 0, wide + ring, wide - ring)
    relay_id = ((sec, flipped, grp), (1 - sec, flipped, grp))

    pos_centre = pltpu.make_async_copy(pos_ref, pos_win.at[pl.ds(lines, lines)], local_sem.at[0])
    pos_centre.start()

    for d, arrived in ((0, has_right), (1, has_left)):
        @pl.when(jnp.logical_not(arrived))
        def _():
            place = pl.ds((1 - d) * 2 * rows, rows)
            partner_win[place, :] = jnp.zeros((rows, partner_win.shape[1]), partner_win.dtype)
            pos_win[pl.ds((1 - d) * 2 * lines, lines), :] = jnp.zeros(pos_ref.shape, jnp.int32)

    greet(relay_id, ((has_left, left_id), (has_right, right_id)))

    def hop(k, p):
        return pltpu.make_async_remote_copy(
            src_ref=own_ref.at[pl.ds(k * half + p * piece, piece)],
            dst_ref=relay.at[k, pl.ds(p * piece, piece)],
            send_sem=hop_send.at[k, p], recv_sem=hop_recv.at[k, p],
            device_id=relay_id[k], device_id_type=MESH_ID)

    def last(k, p):
        return pltpu.make_async_remote_copy(
            src_ref=relay.at[k, pl.ds(p * piece, piece)],
            dst_ref=partner_win.at[pl.ds(rows + k * half + p * piece, piece)],
            send_sem=last_send.at[k, p], recv_sem=last_recv.at[k, p],
            device_id=relay_id[1 - k], device_id_type=MESH_ID)

    def pos_copy(d):
        return pltpu.make_async_remote_copy(
            src_ref=pos_ref,
            dst_ref=pos_win.at[pl.ds((1 - d) * 2 * lines, lines)],
            send_sem=halo_send.at[d], recv_sem=halo_recv.at[d],
            device_id=left_id if d == 0 else right_id, device_id_type=MESH_ID)

    def fwd_copy(d, q):
        return pltpu.make_async_remote_copy(
            src_ref=partner_win.at[pl.ds(rows + q * piece, piece)],
            dst_ref=partner_win.at[pl.ds((1 - d) * 2 * rows + q * piece, piece)],
            send_sem=fwd_send.at[d, q], recv_sem=fwd_recv.at[d, q],
            device_id=left_id if d == 0 else right_id, device_id_type=MESH_ID)

    for p in range(PIECES):
        for k in range(2):
            hop(k, p).start()
    sides = ((0, has_left), (1, has_right))
    for d, present in sides:
        @pl.when(present)
        def _():
            pos_copy(d).start()

    for p in range(PIECES):
        for k in range(2):
            hop(k, p).wait_recv()
            last(k, p).start()
    for p in range(PIECES):
        for k in range(2):
            last(k, p).wait_recv()
            q = k * PIECES + p
            for d, present in sides:
                @pl.when(present)
                def _():
                    fwd_copy(d, q).start()

    for d, present in sides:
        @pl.when(present)
        def _():
            pos_copy(d).wait_send()
            for q in range(2 * PIECES):
                fwd_copy(d, q).wait_send()

        arrived = has_right if d == 0 else has_left

        @pl.when(arrived)
        def _():
            pos_copy(d).wait_recv()
            for q in range(2 * PIECES):
                fwd_copy(d, q).wait_recv()

    for p in range(PIECES):
        for k in range(2):
            hop(k, p).wait_send()
            last(k, p).wait_send()
    pos_centre.wait()
    outs = ((partner_win, partner_out), (pos_win, pos_out))
    copies = [pltpu.make_async_copy(a, b, local_sem.at[1 + n]) for n, (a, b) in enumerate(outs)]
    for copy in copies:
        copy.start()
    for copy in copies:
        copy.wait()


def exchange(own, positives, groups):
    rows, features = own.shape
    lanes = 128
    lined = positives.reshape(rows // lanes, lanes)
    window = jax.ShapeDtypeStruct((3 * rows, features), own.dtype)
    pos_window = jax.ShapeDtypeStruct((3 * rows // lanes, lanes), jnp.int32)
    anywhere = pl.BlockSpec(memory_space=pl.ANY)
    partner_win, pos_win = pl.pallas_call(
        functools.partial(exchange_kernel, groups),
        out_shape=(window, pos_window),
        in_specs=[anywhere, anywhere],
        out_specs=(anywhere, anywhere),
        scratch_shapes=[
            pltpu.VMEM((3 * rows, features), own.dtype),
            pltpu.VMEM((3 * rows // lanes, lanes), jnp.int32),
            pltpu.VMEM((2, rows // 2, features), own.dtype),
            pltpu.SemaphoreType.DMA((3,)),
            pltpu.SemaphoreType.DMA((2, PIECES)),
            pltpu.SemaphoreType.DMA((2, PIECES)),
            pltpu.SemaphoreType.DMA((2, PIECES)),
            pltpu.SemaphoreType.DMA((2, PIECES)),
            pltpu.SemaphoreType.DMA((2, 2 * PIECES)),
            pltpu.SemaphoreType.DMA((2, 2 * PIECES)),
            pltpu.SemaphoreType.DMA((2,)),
            pltpu.SemaphoreType.DMA((2,)),
        ],
        compiler_params=pltpu.CompilerParams(
            collective_id=0, has_side_effects=True, vmem_limit_bytes=32 * 1024 * 1024
        ),
    )(own, lined)
    return partner_win, pos_win.reshape(3 * rows)


def partials_kernel(groups, part_ref, out_ref, held, sems):
    lines = part_ref.shape[0]
    third = lines // 3
    sec, wide, grp, has_left, has_right, left_id, right_id = place_of(groups)
    empty = jnp.full((third, part_ref.shape[1]), -jnp.inf, jnp.float32)
    held[0, pl.ds(2 * third, third), :] = empty
    held[1, pl.ds(0, third), :] = empty

    @pl.when(jnp.logical_not(has_left))
    def _():
        held[0, pl.ds(0, 2 * third), :] = jnp.full((2 * third, part_ref.shape[1]), -jnp.inf)

    @pl.when(jnp.logical_not(has_right))
    def _():
        held[1, pl.ds(third, 2 * third), :] = jnp.full((2 * third, part_ref.shape[1]), -jnp.inf)

    greet((), ((has_left, left_id), (has_right, right_id)))

    def send(d):
        return pltpu.make_async_remote_copy(
            src_ref=part_ref.at[pl.ds(d * third, 2 * third)],
            dst_ref=held.at[1 - d, pl.ds((1 - d) * third, 2 * third)],
            send_sem=sems.at[0, d], recv_sem=sems.at[1, d],
            device_id=left_id if d == 0 else right_id, device_id_type=MESH_ID)

    sides = ((0, has_left), (1, has_right))
    for d, present in sides:
        @pl.when(present)
        def _():
            send(d).start()
    for d, present in sides:
        @pl.when(present)
        def _():
            send(d).wait_send()

        arrived = has_right if d == 0 else has_left

        @pl.when(arrived)
        def _():
            send(d).wait_recv()
    out_ref[...] = held[...]


def neighbour_partials(partial, groups):
    lanes = 128
    lined = partial.reshape(-1, lanes)
    held = pl.pallas_call(
        functools.partial(partials_kernel, groups),
        out_shape=jax.ShapeDtypeStruct((2,) + lined.shape, jnp.float32),
        in_specs=[pl.BlockSpec(memory_space=pltpu.VMEM)],
        out_specs=pl.BlockSpec(memory_space=pltpu.VMEM),
        scratch_shapes=[
            pltpu.VMEM((2,) + lined.shape, jnp.float32),
            pltpu.SemaphoreType.DMA((2, 2)),
        ],
        compiler_params=pltpu.CompilerParams(collective_id=1, has_side_effects=True),
    )(lined)
    return held.reshape(2, -1)


def masked_lse(scores, allowed, axis):
    top = jnp.max(jnp.where(allowed, scores, -jnp.inf), axis=axis, keepdims=True)
    top = jnp.where(jnp.isfinite(top), top, 0.0)
    total = jnp.sum(jnp.where(allowed, jnp.exp(scores - top), 0.0), axis=axis, keepdims=True)
    return jnp.log(total) + top


def local(embeddings, bin_ids, positives):
    own = embeddings[0]
    row_count, features = own.shape
    blocks = row_count // BLOCK
    groups = lax.axis_size("grp")
    me = lax.axis_index(ROWS)
    first_row = me * row_count
    spectral = lax.axis_index("sec") == 0

    partner_win, pos_win = exchange(own, positives, groups)
    win = 3 * row_count

    padded = jnp.pad(bin_ids, blocks, constant_values=-1)
    near_bins = jnp.repeat(lax.dynamic_slice_in_dim(padded, me * blocks, 3 * blocks, 0), BLOCK)
    own_bins = jnp.repeat(lax.dynamic_slice_in_dim(bin_ids, me * blocks, blocks, 0), BLOCK)
    allowed = own_bins[:, None] == near_bins[None, :]

    scores = logit_scale * lax.dot_general(
        own, partner_win, (((1,), (1,)), ((), ())), preferred_element_type=jnp.float32
    )
    own_total = masked_lse(scores, allowed, 1)
    partial = masked_lse(scores, allowed, 0)[0]
    beside = neighbour_partials(partial, groups)
    stacked = jnp.stack([partial, beside[0], beside[1]])
    top = jnp.max(stacked, axis=0)
    top = jnp.where(jnp.isfinite(top), top, 0.0)
    partner_total = (jnp.log(jnp.sum(jnp.exp(stacked - top), axis=0)) + top)[None, :]

    window_index = first_row - row_count + jnp.arange(win, dtype=jnp.int32)
    own_index = first_row + jnp.arange(row_count, dtype=jnp.int32)
    spectra_hits = window_index[None, :] == positives[:, None]
    molecule_hits = pos_win[None, :] == own_index[:, None]
    hits = jnp.where(spectral, spectra_hits, molecule_hits) & allowed
    hits = hits.astype(jnp.float32)

    weights = jnp.exp(scores - own_total) + jnp.exp(scores - partner_total)
    weights = jnp.where(allowed, weights, 0.0) - 2.0 * hits
    grad = logit_scale * jnp.dot(
        weights.astype(jnp.bfloat16), partner_win, preferred_element_type=jnp.float32
    )
    return grad.astype(jnp.bfloat16)[None]


def solution(mesh):
    in_specs = (P("sec", ROWS, None), P(), P(ROWS))
    out_specs = P("sec", ROWS, None)
    return jax.shard_map(local, mesh=mesh, in_specs=in_specs, out_specs=out_specs, check_vma=False)
```

```python
import functools

import jax
import jax.numpy as jnp
from jax import lax
from jax.experimental import pallas as pl
from jax.experimental.pallas import tpu as pltpu
from jax.sharding import PartitionSpec as P

BLOCK = 256
logit_scale = 0.125
ROWS = ("wide", "grp")


MESH_ID = pl.DeviceIdType.MESH
PIECES = 8
IN_FLIGHT = 2


def place_of(groups):
    sec = lax.axis_index("sec")
    wide = lax.axis_index("wide")
    grp = lax.axis_index("grp")
    count = lax.axis_size("wide") * groups
    me = wide * groups + grp
    left_id = (sec, (me - 1) // groups, (me - 1) % groups)
    right_id = (sec, (me + 1) // groups, (me + 1) % groups)
    return sec, wide, grp, me > 0, me < count - 1, left_id, right_id


def greet(peers_always, sides):
    barrier = pltpu.get_barrier_semaphore()
    for peer in peers_always:
        pl.semaphore_signal(barrier, 1, device_id=peer, device_id_type=MESH_ID)
    peers = len(peers_always)
    for present, peer in sides:
        @pl.when(present)
        def _():
            pl.semaphore_signal(barrier, 1, device_id=peer, device_id_type=MESH_ID)

        peers = peers + present.astype(jnp.int32)
    pl.semaphore_wait(barrier, peers)


def exchange_kernel(groups, own_ref, pos_ref, own_bins_ref, near_bins_ref, partner_out, pos_out,
                    own_total_ref, partner_total_ref, partner_win, pos_win, own_rows, partial,
                    held, local_sem, sec_send, sec_recv, fwd_send, fwd_recv, halo_send, halo_recv,
                    part_sems):
    rows = own_ref.shape[0]
    piece = rows // PIECES
    lines = pos_ref.shape[0]
    sec, wide, grp, has_left, has_right, left_id, right_id = place_of(groups)
    partner_id = (1 - sec, wide, grp)

    pos_centre = pltpu.make_async_copy(pos_ref, pos_win.at[pl.ds(lines, lines)], local_sem.at[0])
    pos_centre.start()
    own_copy = pltpu.make_async_copy(own_ref, own_rows, local_sem.at[3])
    own_copy.start()
    win = 3 * rows
    empty = jnp.full((1, rows), -jnp.inf, jnp.float32)
    held[0, :, pl.ds(2 * rows, rows)] = empty
    held[1, :, pl.ds(0, rows)] = empty

    @pl.when(jnp.logical_not(has_left))
    def _():
        held[0, :, pl.ds(0, 2 * rows)] = jnp.full((1, 2 * rows), -jnp.inf, jnp.float32)

    @pl.when(jnp.logical_not(has_right))
    def _():
        held[1, :, pl.ds(rows, 2 * rows)] = jnp.full((1, 2 * rows), -jnp.inf, jnp.float32)

    for d, arrived in ((0, has_right), (1, has_left)):
        @pl.when(jnp.logical_not(arrived))
        def _():
            place = pl.ds((1 - d) * 2 * rows, rows)
            partner_win[place, :] = jnp.zeros((rows, partner_win.shape[1]), partner_win.dtype)
            pos_win[pl.ds((1 - d) * 2 * lines, lines), :] = jnp.zeros(pos_ref.shape, jnp.int32)

    greet((partner_id,), ((has_left, left_id), (has_right, right_id)))

    def sec_copy(q):
        return pltpu.make_async_remote_copy(
            src_ref=own_ref.at[pl.ds(q * piece, piece)],
            dst_ref=partner_win.at[pl.ds(rows + q * piece, piece)],
            send_sem=sec_send.at[q], recv_sem=sec_recv.at[q],
            device_id=partner_id, device_id_type=MESH_ID)

    def pos_copy(d):
        return pltpu.make_async_remote_copy(
            src_ref=pos_ref,
            dst_ref=pos_win.at[pl.ds((1 - d) * 2 * lines, lines)],
            send_sem=halo_send.at[d], recv_sem=halo_recv.at[d],
            device_id=left_id if d == 0 else right_id, device_id_type=MESH_ID)

    def fwd_copy(d, q):
        return pltpu.make_async_remote_copy(
            src_ref=partner_win.at[pl.ds(rows + q * piece, piece)],
            dst_ref=partner_win.at[pl.ds((1 - d) * 2 * rows + q * piece, piece)],
            send_sem=fwd_send.at[d, q], recv_sem=fwd_recv.at[d, q],
            device_id=left_id if d == 0 else right_id, device_id_type=MESH_ID)

    sides = ((0, has_left), (1, has_right))
    for d, present in sides:
        @pl.when(present)
        def _():
            pos_copy(d).start()

    for q in range(IN_FLIGHT):
        sec_copy(q).start()
    for q in range(PIECES):
        sec_copy(q).wait_send()
        if q + IN_FLIGHT < PIECES:
            sec_copy(q + IN_FLIGHT).start()
        sec_copy(q).wait_recv()
        for d, present in sides:
            @pl.when(present)
            def _():
                fwd_copy(d, q).start()

    for d, present in sides:
        @pl.when(present)
        def _():
            pos_copy(d).wait_send()
            for q in range(PIECES):
                fwd_copy(d, q).wait_send()

        arrived = has_right if d == 0 else has_left

        @pl.when(arrived)
        def _():
            pos_copy(d).wait_recv()
            for q in range(PIECES):
                fwd_copy(d, q).wait_recv()

    pos_centre.wait()
    outs = ((partner_win, partner_out), (pos_win, pos_out))
    copies = [pltpu.make_async_copy(a, b, local_sem.at[1 + n]) for n, (a, b) in enumerate(outs)]
    for copy in copies:
        copy.start()

    own_copy.wait()
    scores = logit_scale * lax.dot_general(
        own_rows[...], partner_win[...], (((1,), (1,)), ((), ())),
        preferred_element_type=jnp.float32,
    )
    allowed = own_bins_ref[...] == near_bins_ref[...]
    own_total_ref[...] = masked_lse(scores, allowed, 1)
    partial[...] = masked_lse(scores, allowed, 0)

    def part_copy(d):
        return pltpu.make_async_remote_copy(
            src_ref=partial.at[:, pl.ds(d * rows, 2 * rows)],
            dst_ref=held.at[1 - d, :, pl.ds((1 - d) * rows, 2 * rows)],
            send_sem=part_sems.at[0, d], recv_sem=part_sems.at[1, d],
            device_id=left_id if d == 0 else right_id, device_id_type=MESH_ID)

    for d, present in sides:
        @pl.when(present)
        def _():
            part_copy(d).start()
    for d, present in sides:
        @pl.when(present)
        def _():
            part_copy(d).wait_send()

        arrived = has_right if d == 0 else has_left

        @pl.when(arrived)
        def _():
            part_copy(d).wait_recv()

    mine, left, right = partial[...], held[0], held[1]
    top = jnp.maximum(jnp.maximum(mine, left), right)
    top = jnp.where(top > -jnp.inf, top, 0.0)
    total = jnp.exp(mine - top) + jnp.exp(left - top) + jnp.exp(right - top)
    partner_total_ref[...] = jnp.log(total) + top
    for copy in copies:
        copy.wait()


def exchange(own, positives, own_bins, near_bins, groups):
    rows, features = own.shape
    lanes = 128
    lined = positives.reshape(rows // lanes, lanes)
    window = jax.ShapeDtypeStruct((3 * rows, features), own.dtype)
    pos_window = jax.ShapeDtypeStruct((3 * rows // lanes, lanes), jnp.int32)
    own_total = jax.ShapeDtypeStruct((rows, 1), jnp.float32)
    partner_total = jax.ShapeDtypeStruct((1, 3 * rows), jnp.float32)
    anywhere = pl.BlockSpec(memory_space=pl.ANY)
    vmem = pl.BlockSpec(memory_space=pltpu.VMEM)
    partner_win, pos_win, own_total, partner_total = pl.pallas_call(
        functools.partial(exchange_kernel, groups),
        out_shape=(window, pos_window, own_total, partner_total),
        in_specs=[anywhere, anywhere, vmem, vmem],
        out_specs=(anywhere, anywhere, vmem, vmem),
        scratch_shapes=[
            pltpu.VMEM((3 * rows, features), own.dtype),
            pltpu.VMEM((3 * rows // lanes, lanes), jnp.int32),
            pltpu.VMEM((rows, features), own.dtype),
            pltpu.VMEM((1, 3 * rows), jnp.float32),
            pltpu.VMEM((2, 1, 3 * rows), jnp.float32),
            pltpu.SemaphoreType.DMA((4,)),
            pltpu.SemaphoreType.DMA((PIECES,)),
            pltpu.SemaphoreType.DMA((PIECES,)),
            pltpu.SemaphoreType.DMA((2, PIECES)),
            pltpu.SemaphoreType.DMA((2, PIECES)),
            pltpu.SemaphoreType.DMA((2,)),
            pltpu.SemaphoreType.DMA((2,)),
            pltpu.SemaphoreType.DMA((2, 2)),
        ],
        compiler_params=pltpu.CompilerParams(
            collective_id=0, has_side_effects=True, vmem_limit_bytes=48 * 1024 * 1024
        ),
    )(own, lined, own_bins, near_bins)
    return partner_win, pos_win.reshape(3 * rows), own_total, partner_total


def masked_lse(scores, allowed, axis):
    top = jnp.max(jnp.where(allowed, scores, -jnp.inf), axis=axis, keepdims=True)
    top = jnp.where(top > -jnp.inf, top, 0.0)
    total = jnp.sum(jnp.where(allowed, jnp.exp(scores - top), 0.0), axis=axis, keepdims=True)
    return jnp.log(total) + top


def local(embeddings, bin_ids, positives):
    own = embeddings[0]
    row_count, features = own.shape
    blocks = row_count // BLOCK
    groups = lax.axis_size("grp")
    me = lax.axis_index(ROWS)
    first_row = me * row_count
    spectral = lax.axis_index("sec") == 0

    win = 3 * row_count

    padded = jnp.pad(bin_ids, blocks, constant_values=-1)
    near_bins = jnp.repeat(lax.dynamic_slice_in_dim(padded, me * blocks, 3 * blocks, 0), BLOCK)
    own_bins = jnp.repeat(lax.dynamic_slice_in_dim(bin_ids, me * blocks, blocks, 0), BLOCK)
    own_bins = own_bins[:, None]
    near_bins = near_bins[None, :]
    partner_win, pos_win, own_total, partner_total = exchange(
        own, positives, own_bins, near_bins, groups
    )

    window_index = first_row - row_count + jnp.arange(win, dtype=jnp.int32)
    own_index = first_row + jnp.arange(row_count, dtype=jnp.int32)
    spectra_hits = window_index[None, :] == positives[:, None]
    molecule_hits = pos_win[None, :] == own_index[:, None]
    allowed = own_bins == near_bins
    hits = jnp.where(spectral, spectra_hits, molecule_hits) & allowed
    hits = hits.astype(jnp.float32)

    scores = logit_scale * lax.dot_general(
        own, partner_win, (((1,), (1,)), ((), ())), preferred_element_type=jnp.float32
    )
    weights = jnp.exp(scores - own_total) + jnp.exp(scores - partner_total)
    weights = jnp.where(allowed, weights, 0.0) - 2.0 * hits
    grad = logit_scale * jnp.dot(
        weights.astype(jnp.bfloat16), partner_win, preferred_element_type=jnp.float32
    )
    return grad.astype(jnp.bfloat16)[None]


def solution(mesh):
    in_specs = (P("sec", ROWS, None), P(), P(ROWS))
    out_specs = P("sec", ROWS, None)
    return jax.shard_map(local, mesh=mesh, in_specs=in_specs, out_specs=out_specs, check_vma=False)
```

```python
import functools

import jax
import jax.numpy as jnp
from jax import lax
from jax.experimental import pallas as pl
from jax.experimental.pallas import tpu as pltpu
from jax.sharding import PartitionSpec as P

BLOCK = 256
logit_scale = 0.125
ROWS = ("wide", "grp")


MESH_ID = pl.DeviceIdType.MESH
PIECES = 8
IN_FLIGHT = 2


def place_of(groups):
    sec = lax.axis_index("sec")
    wide = lax.axis_index("wide")
    grp = lax.axis_index("grp")
    count = lax.axis_size("wide") * groups
    me = wide * groups + grp
    left_id = (sec, (me - 1) // groups, (me - 1) % groups)
    right_id = (sec, (me + 1) // groups, (me + 1) % groups)
    return sec, wide, grp, me > 0, me < count - 1, left_id, right_id


def greet(peers_always, sides):
    barrier = pltpu.get_barrier_semaphore()
    for peer in peers_always:
        pl.semaphore_signal(barrier, 1, device_id=peer, device_id_type=MESH_ID)
    peers = len(peers_always)
    for present, peer in sides:
        @pl.when(present)
        def _():
            pl.semaphore_signal(barrier, 1, device_id=peer, device_id_type=MESH_ID)

        peers = peers + present.astype(jnp.int32)
    pl.semaphore_wait(barrier, peers)


def exchange_kernel(groups, own_ref, pos_ref, own_bins_ref, near_bins_ref, row_key_ref,
                    window_key_ref, grad_ref, partner_win, pos_win, own_rows, partial, held,
                    local_sem, sec_send, sec_recv, fwd_send, fwd_recv, halo_send, halo_recv,
                    part_sems):
    rows = own_ref.shape[0]
    piece = rows // PIECES
    sec, wide, grp, has_left, has_right, left_id, right_id = place_of(groups)
    partner_id = (1 - sec, wide, grp)

    pos_win[:, pl.ds(rows, rows)] = pos_ref[...]
    own_copy = pltpu.make_async_copy(own_ref, own_rows, local_sem.at[3])
    own_copy.start()
    win = 3 * rows
    empty = jnp.full((1, rows), -jnp.inf, jnp.float32)
    held[0, :, pl.ds(2 * rows, rows)] = empty
    held[1, :, pl.ds(0, rows)] = empty

    @pl.when(jnp.logical_not(has_left))
    def _():
        held[0, :, pl.ds(0, 2 * rows)] = jnp.full((1, 2 * rows), -jnp.inf, jnp.float32)

    @pl.when(jnp.logical_not(has_right))
    def _():
        held[1, :, pl.ds(rows, 2 * rows)] = jnp.full((1, 2 * rows), -jnp.inf, jnp.float32)

    for d, arrived in ((0, has_right), (1, has_left)):
        @pl.when(jnp.logical_not(arrived))
        def _():
            place = pl.ds((1 - d) * 2 * rows, rows)
            partner_win[place, :] = jnp.zeros((rows, partner_win.shape[1]), partner_win.dtype)
            pos_win[:, pl.ds((1 - d) * 2 * rows, rows)] = jnp.zeros(pos_ref.shape, jnp.int32)

    greet((partner_id,), ((has_left, left_id), (has_right, right_id)))

    def sec_copy(q):
        return pltpu.make_async_remote_copy(
            src_ref=own_ref.at[pl.ds(q * piece, piece)],
            dst_ref=partner_win.at[pl.ds(rows + q * piece, piece)],
            send_sem=sec_send.at[q], recv_sem=sec_recv.at[q],
            device_id=partner_id, device_id_type=MESH_ID)

    def pos_copy(d):
        return pltpu.make_async_remote_copy(
            src_ref=pos_ref,
            dst_ref=pos_win.at[:, pl.ds((1 - d) * 2 * rows, rows)],
            send_sem=halo_send.at[d], recv_sem=halo_recv.at[d],
            device_id=left_id if d == 0 else right_id, device_id_type=MESH_ID)

    def fwd_copy(d, q):
        return pltpu.make_async_remote_copy(
            src_ref=partner_win.at[pl.ds(rows + q * piece, piece)],
            dst_ref=partner_win.at[pl.ds((1 - d) * 2 * rows + q * piece, piece)],
            send_sem=fwd_send.at[d, q], recv_sem=fwd_recv.at[d, q],
            device_id=left_id if d == 0 else right_id, device_id_type=MESH_ID)

    sides = ((0, has_left), (1, has_right))
    for d, present in sides:
        @pl.when(present)
        def _():
            pos_copy(d).start()

    for q in range(IN_FLIGHT):
        sec_copy(q).start()
    for q in range(PIECES):
        sec_copy(q).wait_send()
        if q + IN_FLIGHT < PIECES:
            sec_copy(q + IN_FLIGHT).start()
        sec_copy(q).wait_recv()
        for d, present in sides:
            @pl.when(present)
            def _():
                fwd_copy(d, q).start()

    for d, present in sides:
        @pl.when(present)
        def _():
            pos_copy(d).wait_send()
            for q in range(PIECES):
                fwd_copy(d, q).wait_send()

        arrived = has_right if d == 0 else has_left

        @pl.when(arrived)
        def _():
            pos_copy(d).wait_recv()
            for q in range(PIECES):
                fwd_copy(d, q).wait_recv()

    own_copy.wait()
    scores = logit_scale * lax.dot_general(
        own_rows[...], partner_win[...], (((1,), (1,)), ((), ())),
        preferred_element_type=jnp.float32,
    )
    allowed = own_bins_ref[...] == near_bins_ref[...]
    own_total = masked_lse(scores, allowed, 1)
    partial[...] = masked_lse(scores, allowed, 0)

    def part_copy(d):
        return pltpu.make_async_remote_copy(
            src_ref=partial.at[:, pl.ds(d * rows, 2 * rows)],
            dst_ref=held.at[1 - d, :, pl.ds((1 - d) * rows, 2 * rows)],
            send_sem=part_sems.at[0, d], recv_sem=part_sems.at[1, d],
            device_id=left_id if d == 0 else right_id, device_id_type=MESH_ID)

    for d, present in sides:
        @pl.when(present)
        def _():
            part_copy(d).start()
    for d, present in sides:
        @pl.when(present)
        def _():
            part_copy(d).wait_send()

        arrived = has_right if d == 0 else has_left

        @pl.when(arrived)
        def _():
            part_copy(d).wait_recv()

    mine, left, right = partial[...], held[0], held[1]
    top = jnp.maximum(jnp.maximum(mine, left), right)
    top = jnp.where(top > -jnp.inf, top, 0.0)
    total = jnp.exp(mine - top) + jnp.exp(left - top) + jnp.exp(right - top)
    partner_total = jnp.log(total) + top

    col_key = jnp.where(sec == 0, window_key_ref[...], pos_win[...])
    hits = allowed & (row_key_ref[...] == col_key)
    weights = jnp.exp(scores - own_total) + jnp.exp(scores - partner_total)
    weights = jnp.where(allowed, weights, 0.0) - jnp.where(hits, 2.0, 0.0)
    grad = jnp.dot(weights.astype(jnp.bfloat16), partner_win[...], preferred_element_type=jnp.float32)
    grad_ref[...] = (logit_scale * grad).astype(grad_ref.dtype)


def exchange(own, positives, own_bins, near_bins, row_key, window_key, groups):
    rows, features = own.shape
    anywhere = pl.BlockSpec(memory_space=pl.ANY)
    vmem = pl.BlockSpec(memory_space=pltpu.VMEM)
    return pl.pallas_call(
        functools.partial(exchange_kernel, groups),
        out_shape=jax.ShapeDtypeStruct((rows, features), own.dtype),
        in_specs=[anywhere] + [vmem] * 5,
        out_specs=vmem,
        scratch_shapes=[
            pltpu.VMEM((3 * rows, features), own.dtype),
            pltpu.VMEM((1, 3 * rows), jnp.int32),
            pltpu.VMEM((rows, features), own.dtype),
            pltpu.VMEM((1, 3 * rows), jnp.float32),
            pltpu.VMEM((2, 1, 3 * rows), jnp.float32),
            pltpu.SemaphoreType.DMA((4,)),
            pltpu.SemaphoreType.DMA((PIECES,)),
            pltpu.SemaphoreType.DMA((PIECES,)),
            pltpu.SemaphoreType.DMA((2, PIECES)),
            pltpu.SemaphoreType.DMA((2, PIECES)),
            pltpu.SemaphoreType.DMA((2,)),
            pltpu.SemaphoreType.DMA((2,)),
            pltpu.SemaphoreType.DMA((2, 2)),
        ],
        compiler_params=pltpu.CompilerParams(
            collective_id=0, has_side_effects=True, vmem_limit_bytes=48 * 1024 * 1024
        ),
    )(own, positives[None, :], own_bins, near_bins, row_key, window_key)


def masked_lse(scores, allowed, axis):
    top = jnp.max(jnp.where(allowed, scores, -jnp.inf), axis=axis, keepdims=True)
    top = jnp.where(top > -jnp.inf, top, 0.0)
    total = jnp.sum(jnp.where(allowed, jnp.exp(scores - top), 0.0), axis=axis, keepdims=True)
    return jnp.log(total) + top


def local(embeddings, bin_ids, positives):
    own = embeddings[0]
    row_count, features = own.shape
    blocks = row_count // BLOCK
    groups = lax.axis_size("grp")
    me = lax.axis_index(ROWS)
    first_row = me * row_count
    spectral = lax.axis_index("sec") == 0

    win = 3 * row_count

    padded = jnp.pad(bin_ids, blocks, constant_values=-1)
    near_bins = jnp.repeat(lax.dynamic_slice_in_dim(padded, me * blocks, 3 * blocks, 0), BLOCK)
    own_bins = jnp.repeat(lax.dynamic_slice_in_dim(bin_ids, me * blocks, blocks, 0), BLOCK)
    own_bins = own_bins[:, None]
    near_bins = near_bins[None, :]
    window_index = first_row - row_count + jnp.arange(win, dtype=jnp.int32)
    own_index = first_row + jnp.arange(row_count, dtype=jnp.int32)
    row_key = jnp.where(spectral, positives, own_index)[:, None]
    grad = exchange(own, positives, own_bins, near_bins, row_key, window_index[None, :], groups)
    return grad[None]


def solution(mesh):
    in_specs = (P("sec", ROWS, None), P(), P(ROWS))
    out_specs = P("sec", ROWS, None)
    return jax.shard_map(local, mesh=mesh, in_specs=in_specs, out_specs=out_specs, check_vma=False)
```

```python
import functools

import jax
import jax.numpy as jnp
from jax import lax
from jax.experimental import pallas as pl
from jax.experimental.pallas import tpu as pltpu
from jax.sharding import PartitionSpec as P

BLOCK = 256
logit_scale = 0.125
ROWS = ("wide", "grp")


MESH_ID = pl.DeviceIdType.MESH
PIECES = 8
IN_FLIGHT = 2


def place_of(groups):
    sec = lax.axis_index("sec")
    wide = lax.axis_index("wide")
    grp = lax.axis_index("grp")
    count = lax.axis_size("wide") * groups
    me = wide * groups + grp
    left = jnp.maximum(me - 1, 0)
    right = jnp.minimum(me + 1, count - 1)
    left_id = (sec, left // groups, left % groups)
    right_id = (sec, right // groups, right % groups)
    return sec, wide, grp, me > 0, me < count - 1, left_id, right_id


def greet(peers_always, sides):
    barrier = pltpu.get_barrier_semaphore()
    for peer in peers_always:
        pl.semaphore_signal(barrier, 1, device_id=peer, device_id_type=MESH_ID)
    peers = len(peers_always)
    for present, peer in sides:
        @pl.when(present)
        def _():
            pl.semaphore_signal(barrier, 1, device_id=peer, device_id_type=MESH_ID)

        peers = peers + present.astype(jnp.int32)
    pl.semaphore_wait(barrier, peers)


def exchange_kernel(groups, own_ref, pos_ref, own_bins_ref, near_bins_ref, row_key_ref,
                    window_key_ref, grad_ref, partner_win, pos_win, own_rows, partial, held,
                    local_sem, sec_send, sec_recv, fwd_send, fwd_recv, halo_send, halo_recv,
                    part_sems):
    rows = own_ref.shape[0]
    piece = rows // PIECES
    sec, wide, grp, has_left, has_right, left_id, right_id = place_of(groups)
    partner_id = (1 - sec, wide, grp)

    pos_win[:, pl.ds(rows, rows)] = pos_ref[...]
    own_copy = pltpu.make_async_copy(own_ref, own_rows, local_sem.at[3])
    own_copy.start()
    win = 3 * rows
    empty = jnp.full((1, rows), -jnp.inf, jnp.float32)
    held[0, :, pl.ds(2 * rows, rows)] = empty
    held[1, :, pl.ds(0, rows)] = empty

    @pl.when(jnp.logical_not(has_left))
    def _():
        held[0, :, pl.ds(0, 2 * rows)] = jnp.full((1, 2 * rows), -jnp.inf, jnp.float32)

    @pl.when(jnp.logical_not(has_right))
    def _():
        held[1, :, pl.ds(rows, 2 * rows)] = jnp.full((1, 2 * rows), -jnp.inf, jnp.float32)

    for d, arrived in ((0, has_right), (1, has_left)):
        @pl.when(jnp.logical_not(arrived))
        def _():
            place = pl.ds((1 - d) * 2 * rows, rows)
            partner_win[place, :] = jnp.zeros((rows, partner_win.shape[1]), partner_win.dtype)
            pos_win[:, pl.ds((1 - d) * 2 * rows, rows)] = jnp.zeros(pos_ref.shape, jnp.int32)

    greet((partner_id,), ((has_left, left_id), (has_right, right_id)))

    def sec_copy(q):
        return pltpu.make_async_remote_copy(
            src_ref=own_ref.at[pl.ds(q * piece, piece)],
            dst_ref=partner_win.at[pl.ds(rows + q * piece, piece)],
            send_sem=sec_send.at[q], recv_sem=sec_recv.at[q],
            device_id=partner_id, device_id_type=MESH_ID)

    def pos_copy(d):
        return pltpu.make_async_remote_copy(
            src_ref=pos_ref,
            dst_ref=pos_win.at[:, pl.ds((1 - d) * 2 * rows, rows)],
            send_sem=halo_send.at[d], recv_sem=halo_recv.at[d],
            device_id=left_id if d == 0 else right_id, device_id_type=MESH_ID)

    def fwd_copy(d, q):
        return pltpu.make_async_remote_copy(
            src_ref=partner_win.at[pl.ds(rows + q * piece, piece)],
            dst_ref=partner_win.at[pl.ds((1 - d) * 2 * rows + q * piece, piece)],
            send_sem=fwd_send.at[d, q], recv_sem=fwd_recv.at[d, q],
            device_id=left_id if d == 0 else right_id, device_id_type=MESH_ID)

    sides = ((0, has_left), (1, has_right))
    for d, present in sides:
        @pl.when(present)
        def _():
            pos_copy(d).start()

    for q in range(IN_FLIGHT):
        sec_copy(q).start()
    for q in range(PIECES):
        sec_copy(q).wait_send()
        if q + IN_FLIGHT < PIECES:
            sec_copy(q + IN_FLIGHT).start()
        sec_copy(q).wait_recv()
        for d, present in sides:
            @pl.when(present)
            def _():
                fwd_copy(d, q).start()

    for d, present in sides:
        @pl.when(present)
        def _():
            pos_copy(d).wait_send()
            for q in range(PIECES):
                fwd_copy(d, q).wait_send()

        arrived = has_right if d == 0 else has_left

        @pl.when(arrived)
        def _():
            pos_copy(d).wait_recv()
            for q in range(PIECES):
                fwd_copy(d, q).wait_recv()

    own_copy.wait()
    scores = logit_scale * lax.dot_general(
        own_rows[...], partner_win[...], (((1,), (1,)), ((), ())),
        preferred_element_type=jnp.float32,
    )
    allowed = own_bins_ref[...] == near_bins_ref[...]
    own_total = masked_lse(scores, allowed, 1)
    partial[...] = masked_lse(scores, allowed, 0)

    def part_copy(d):
        return pltpu.make_async_remote_copy(
            src_ref=partial.at[:, pl.ds(d * rows, 2 * rows)],
            dst_ref=held.at[1 - d, :, pl.ds((1 - d) * rows, 2 * rows)],
            send_sem=part_sems.at[0, d], recv_sem=part_sems.at[1, d],
            device_id=left_id if d == 0 else right_id, device_id_type=MESH_ID)

    for d, present in sides:
        @pl.when(present)
        def _():
            part_copy(d).start()
    for d, present in sides:
        @pl.when(present)
        def _():
            part_copy(d).wait_send()

        arrived = has_right if d == 0 else has_left

        @pl.when(arrived)
        def _():
            part_copy(d).wait_recv()

    mine, left, right = partial[...], held[0], held[1]
    top = jnp.maximum(jnp.maximum(mine, left), right)
    top = jnp.where(top > -jnp.inf, top, 0.0)
    total = jnp.exp(mine - top) + jnp.exp(left - top) + jnp.exp(right - top)
    partner_total = jnp.log(total) + top

    col_key = jnp.where(sec == 0, window_key_ref[...], pos_win[...])
    hits = allowed & (row_key_ref[...] == col_key)
    weights = jnp.exp(scores - own_total) + jnp.exp(scores - partner_total)
    weights = jnp.where(allowed, weights, 0.0) - jnp.where(hits, 2.0, 0.0)
    grad = jnp.dot(weights.astype(jnp.bfloat16), partner_win[...], preferred_element_type=jnp.float32)
    grad_ref[...] = (logit_scale * grad).astype(grad_ref.dtype)


def exchange(own, positives, own_bins, near_bins, row_key, window_key, groups):
    rows, features = own.shape
    anywhere = pl.BlockSpec(memory_space=pl.ANY)
    vmem = pl.BlockSpec(memory_space=pltpu.VMEM)
    return pl.pallas_call(
        functools.partial(exchange_kernel, groups),
        out_shape=jax.ShapeDtypeStruct((rows, features), own.dtype),
        in_specs=[anywhere] + [vmem] * 5,
        out_specs=vmem,
        scratch_shapes=[
            pltpu.VMEM((3 * rows, features), own.dtype),
            pltpu.VMEM((1, 3 * rows), jnp.int32),
            pltpu.VMEM((rows, features), own.dtype),
            pltpu.VMEM((1, 3 * rows), jnp.float32),
            pltpu.VMEM((2, 1, 3 * rows), jnp.float32),
            pltpu.SemaphoreType.DMA((4,)),
            pltpu.SemaphoreType.DMA((PIECES,)),
            pltpu.SemaphoreType.DMA((PIECES,)),
            pltpu.SemaphoreType.DMA((2, PIECES)),
            pltpu.SemaphoreType.DMA((2, PIECES)),
            pltpu.SemaphoreType.DMA((2,)),
            pltpu.SemaphoreType.DMA((2,)),
            pltpu.SemaphoreType.DMA((2, 2)),
        ],
        compiler_params=pltpu.CompilerParams(
            collective_id=0, has_side_effects=True, vmem_limit_bytes=48 * 1024 * 1024
        ),
    )(own, positives[None, :], own_bins, near_bins, row_key, window_key)


def masked_lse(scores, allowed, axis):
    top = jnp.max(jnp.where(allowed, scores, -jnp.inf), axis=axis, keepdims=True)
    top = jnp.where(top > -jnp.inf, top, 0.0)
    total = jnp.sum(jnp.where(allowed, jnp.exp(scores - top), 0.0), axis=axis, keepdims=True)
    return jnp.log(total) + top


def local(embeddings, bin_ids, positives):
    own = embeddings[0]
    row_count, features = own.shape
    blocks = row_count // BLOCK
    groups = lax.axis_size("grp")
    me = lax.axis_index(ROWS)
    first_row = me * row_count
    spectral = lax.axis_index("sec") == 0

    win = 3 * row_count

    padded = jnp.pad(bin_ids, blocks, constant_values=-1)
    near_bins = jnp.repeat(lax.dynamic_slice_in_dim(padded, me * blocks, 3 * blocks, 0), BLOCK)
    own_bins = jnp.repeat(lax.dynamic_slice_in_dim(bin_ids, me * blocks, blocks, 0), BLOCK)
    own_bins = own_bins[:, None]
    near_bins = near_bins[None, :]
    window_index = first_row - row_count + jnp.arange(win, dtype=jnp.int32)
    own_index = first_row + jnp.arange(row_count, dtype=jnp.int32)
    row_key = jnp.where(spectral, positives, own_index)[:, None]
    grad = exchange(own, positives, own_bins, near_bins, row_key, window_index[None, :], groups)
    return grad[None]


def solution(mesh):
    in_specs = (P("sec", ROWS, None), P(), P(ROWS))
    out_specs = P("sec", ROWS, None)
    return jax.shard_map(local, mesh=mesh, in_specs=in_specs, out_specs=out_specs, check_vma=False)
```

```python
import functools

import jax
import jax.numpy as jnp
from jax import lax
from jax.experimental import pallas as pl
from jax.experimental.pallas import tpu as pltpu
from jax.sharding import PartitionSpec as P

BLOCK = 256
logit_scale = 0.125
ROWS = ("wide", "grp")


MESH_ID = pl.DeviceIdType.MESH
PIECES = 8
IN_FLIGHT = 2
Y_CHIPS = 8


def place_of(groups):
    sec = lax.axis_index("sec")
    wide = lax.axis_index("wide")
    grp = lax.axis_index("grp")
    count = lax.axis_size("wide") * groups
    me = wide * groups + grp
    left = jnp.maximum(me - 1, 0)
    right = jnp.minimum(me + 1, count - 1)
    left_id = (sec, left // groups, left % groups)
    right_id = (sec, right // groups, right % groups)
    return sec, wide, grp, me > 0, me < count - 1, left_id, right_id


def greet(peers_always, sides):
    barrier = pltpu.get_barrier_semaphore()
    for peer in peers_always:
        pl.semaphore_signal(barrier, 1, device_id=peer, device_id_type=MESH_ID)
    peers = len(peers_always)
    for present, peer in sides:
        @pl.when(present)
        def _():
            pl.semaphore_signal(barrier, 1, device_id=peer, device_id_type=MESH_ID)

        peers = peers + present.astype(jnp.int32)
    pl.semaphore_wait(barrier, peers)


def exchange_kernel(groups, own_ref, pos_ref, own_bins_ref, near_bins_ref, row_key_ref,
                    window_key_ref, grad_ref, partner_win, pos_win, own_rows, partial, held,
                    local_sem, sec_send, sec_recv, fwd_send, fwd_recv, halo_send, halo_recv,
                    part_sems):
    rows = own_ref.shape[0]
    piece = rows // PIECES
    sec, wide, grp, has_left, has_right, left_id, right_id = place_of(groups)
    partner_id = (1 - sec, wide, grp)
    me = wide * groups + grp
    left_cross = has_left & ((me - 1) // groups // Y_CHIPS != wide // Y_CHIPS)
    right_cross = has_right & ((me + 1) // groups // Y_CHIPS != wide // Y_CHIPS)
    cross = (left_cross, right_cross)
    across_id = tuple((1 - sec,) + tuple(peer[1:]) for peer in (left_id, right_id))

    pos_win[:, pl.ds(rows, rows)] = pos_ref[...]
    own_copy = pltpu.make_async_copy(own_ref, own_rows, local_sem.at[3])
    own_copy.start()
    win = 3 * rows
    empty = jnp.full((1, rows), -jnp.inf, jnp.float32)
    held[0, :, pl.ds(2 * rows, rows)] = empty
    held[1, :, pl.ds(0, rows)] = empty

    @pl.when(jnp.logical_not(has_left))
    def _():
        held[0, :, pl.ds(0, 2 * rows)] = jnp.full((1, 2 * rows), -jnp.inf, jnp.float32)

    @pl.when(jnp.logical_not(has_right))
    def _():
        held[1, :, pl.ds(rows, 2 * rows)] = jnp.full((1, 2 * rows), -jnp.inf, jnp.float32)

    for d, arrived in ((0, has_right), (1, has_left)):
        @pl.when(jnp.logical_not(arrived))
        def _():
            place = pl.ds((1 - d) * 2 * rows, rows)
            partner_win[place, :] = jnp.zeros((rows, partner_win.shape[1]), partner_win.dtype)
            pos_win[:, pl.ds((1 - d) * 2 * rows, rows)] = jnp.zeros(pos_ref.shape, jnp.int32)

    greet((partner_id,), ((has_left, left_id), (has_right, right_id),
                          (left_cross, across_id[0]), (right_cross, across_id[1])))

    def sec_copy(q):
        return pltpu.make_async_remote_copy(
            src_ref=own_ref.at[pl.ds(q * piece, piece)],
            dst_ref=partner_win.at[pl.ds(rows + q * piece, piece)],
            send_sem=sec_send.at[q], recv_sem=sec_recv.at[q],
            device_id=partner_id, device_id_type=MESH_ID)

    def pos_copy(d):
        return pltpu.make_async_remote_copy(
            src_ref=pos_ref,
            dst_ref=pos_win.at[:, pl.ds((1 - d) * 2 * rows, rows)],
            send_sem=halo_send.at[d], recv_sem=halo_recv.at[d],
            device_id=left_id if d == 0 else right_id, device_id_type=MESH_ID)

    def fwd_copy(d, q):
        return pltpu.make_async_remote_copy(
            src_ref=partner_win.at[pl.ds(rows + q * piece, piece)],
            dst_ref=partner_win.at[pl.ds((1 - d) * 2 * rows + q * piece, piece)],
            send_sem=fwd_send.at[d, q], recv_sem=fwd_recv.at[d, q],
            device_id=left_id if d == 0 else right_id, device_id_type=MESH_ID)

    def cross_copy(d, q):
        return pltpu.make_async_remote_copy(
            src_ref=own_ref.at[pl.ds(q * piece, piece)],
            dst_ref=partner_win.at[pl.ds((1 - d) * 2 * rows + q * piece, piece)],
            send_sem=fwd_send.at[d, q], recv_sem=fwd_recv.at[d, q],
            device_id=across_id[d], device_id_type=MESH_ID)

    sides = ((0, has_left), (1, has_right))
    for d, present in sides:
        @pl.when(present)
        def _():
            pos_copy(d).start()

        @pl.when(cross[d])
        def _():
            for q in range(PIECES):
                cross_copy(d, q).start()

    for q in range(IN_FLIGHT):
        sec_copy(q).start()
    for q in range(PIECES):
        sec_copy(q).wait_send()
        if q + IN_FLIGHT < PIECES:
            sec_copy(q + IN_FLIGHT).start()
        sec_copy(q).wait_recv()
        for d, present in sides:
            @pl.when(present & jnp.logical_not(cross[d]))
            def _():
                fwd_copy(d, q).start()

    for d, present in sides:
        @pl.when(present)
        def _():
            pos_copy(d).wait_send()

        @pl.when(present & jnp.logical_not(cross[d]))
        def _():
            for q in range(PIECES):
                fwd_copy(d, q).wait_send()

        @pl.when(cross[d])
        def _():
            for q in range(PIECES):
                cross_copy(d, q).wait_send()

        arrived = has_right if d == 0 else has_left

        @pl.when(arrived)
        def _():
            pos_copy(d).wait_recv()
            for q in range(PIECES):
                fwd_copy(d, q).wait_recv()

    own_copy.wait()
    scores = logit_scale * lax.dot_general(
        own_rows[...], partner_win[...], (((1,), (1,)), ((), ())),
        preferred_element_type=jnp.float32,
    )
    allowed = own_bins_ref[...] == near_bins_ref[...]
    own_total = masked_lse(scores, allowed, 1)
    partial[...] = masked_lse(scores, allowed, 0)

    def part_copy(d):
        return pltpu.make_async_remote_copy(
            src_ref=partial.at[:, pl.ds(d * rows, 2 * rows)],
            dst_ref=held.at[1 - d, :, pl.ds((1 - d) * rows, 2 * rows)],
            send_sem=part_sems.at[0, d], recv_sem=part_sems.at[1, d],
            device_id=left_id if d == 0 else right_id, device_id_type=MESH_ID)

    for d, present in sides:
        @pl.when(present)
        def _():
            part_copy(d).start()
    for d, present in sides:
        @pl.when(present)
        def _():
            part_copy(d).wait_send()

        arrived = has_right if d == 0 else has_left

        @pl.when(arrived)
        def _():
            part_copy(d).wait_recv()

    mine, left, right = partial[...], held[0], held[1]
    top = jnp.maximum(jnp.maximum(mine, left), right)
    top = jnp.where(top > -jnp.inf, top, 0.0)
    total = jnp.exp(mine - top) + jnp.exp(left - top) + jnp.exp(right - top)
    partner_total = jnp.log(total) + top

    col_key = jnp.where(sec == 0, window_key_ref[...], pos_win[...])
    hits = allowed & (row_key_ref[...] == col_key)
    weights = jnp.exp(scores - own_total) + jnp.exp(scores - partner_total)
    weights = jnp.where(allowed, weights, 0.0) - jnp.where(hits, 2.0, 0.0)
    grad = jnp.dot(weights.astype(jnp.bfloat16), partner_win[...], preferred_element_type=jnp.float32)
    grad_ref[...] = (logit_scale * grad).astype(grad_ref.dtype)


def exchange(own, positives, own_bins, near_bins, row_key, window_key, groups):
    rows, features = own.shape
    anywhere = pl.BlockSpec(memory_space=pl.ANY)
    vmem = pl.BlockSpec(memory_space=pltpu.VMEM)
    return pl.pallas_call(
        functools.partial(exchange_kernel, groups),
        out_shape=jax.ShapeDtypeStruct((rows, features), own.dtype),
        in_specs=[anywhere] + [vmem] * 5,
        out_specs=vmem,
        scratch_shapes=[
            pltpu.VMEM((3 * rows, features), own.dtype),
            pltpu.VMEM((1, 3 * rows), jnp.int32),
            pltpu.VMEM((rows, features), own.dtype),
            pltpu.VMEM((1, 3 * rows), jnp.float32),
            pltpu.VMEM((2, 1, 3 * rows), jnp.float32),
            pltpu.SemaphoreType.DMA((4,)),
            pltpu.SemaphoreType.DMA((PIECES,)),
            pltpu.SemaphoreType.DMA((PIECES,)),
            pltpu.SemaphoreType.DMA((2, PIECES)),
            pltpu.SemaphoreType.DMA((2, PIECES)),
            pltpu.SemaphoreType.DMA((2,)),
            pltpu.SemaphoreType.DMA((2,)),
            pltpu.SemaphoreType.DMA((2, 2)),
        ],
        compiler_params=pltpu.CompilerParams(
            collective_id=0, has_side_effects=True, vmem_limit_bytes=48 * 1024 * 1024
        ),
    )(own, positives[None, :], own_bins, near_bins, row_key, window_key)


def masked_lse(scores, allowed, axis):
    top = jnp.max(jnp.where(allowed, scores, -jnp.inf), axis=axis, keepdims=True)
    top = jnp.where(top > -jnp.inf, top, 0.0)
    total = jnp.sum(jnp.where(allowed, jnp.exp(scores - top), 0.0), axis=axis, keepdims=True)
    return jnp.log(total) + top


def local(embeddings, bin_ids, positives):
    own = embeddings[0]
    row_count, features = own.shape
    blocks = row_count // BLOCK
    groups = lax.axis_size("grp")
    me = lax.axis_index(ROWS)
    first_row = me * row_count
    spectral = lax.axis_index("sec") == 0

    win = 3 * row_count

    padded = jnp.pad(bin_ids, blocks, constant_values=-1)
    near_bins = jnp.repeat(lax.dynamic_slice_in_dim(padded, me * blocks, 3 * blocks, 0), BLOCK)
    own_bins = jnp.repeat(lax.dynamic_slice_in_dim(bin_ids, me * blocks, blocks, 0), BLOCK)
    own_bins = own_bins[:, None]
    near_bins = near_bins[None, :]
    window_index = first_row - row_count + jnp.arange(win, dtype=jnp.int32)
    own_index = first_row + jnp.arange(row_count, dtype=jnp.int32)
    row_key = jnp.where(spectral, positives, own_index)[:, None]
    grad = exchange(own, positives, own_bins, near_bins, row_key, window_index[None, :], groups)
    return grad[None]


def solution(mesh):
    in_specs = (P("sec", ROWS, None), P(), P(ROWS))
    out_specs = P("sec", ROWS, None)
    return jax.shard_map(local, mesh=mesh, in_specs=in_specs, out_specs=out_specs, check_vma=False)
```

```python
import functools

import jax
import jax.numpy as jnp
from jax import lax
from jax.experimental import pallas as pl
from jax.experimental.pallas import tpu as pltpu
from jax.sharding import PartitionSpec as P

BLOCK = 256
logit_scale = 0.125
ROWS = ("wide", "grp")


MESH_ID = pl.DeviceIdType.MESH
PIECES = 8
IN_FLIGHT = 2
Y_CHIPS = 8
SPLIT = PIECES // 2


def place_of(groups):
    sec = lax.axis_index("sec")
    wide = lax.axis_index("wide")
    grp = lax.axis_index("grp")
    count = lax.axis_size("wide") * groups
    me = wide * groups + grp
    left = jnp.maximum(me - 1, 0)
    right = jnp.minimum(me + 1, count - 1)
    left_id = (sec, left // groups, left % groups)
    right_id = (sec, right // groups, right % groups)
    return sec, wide, grp, me > 0, me < count - 1, left_id, right_id


def greet(peers_always, sides):
    barrier = pltpu.get_barrier_semaphore()
    for peer in peers_always:
        pl.semaphore_signal(barrier, 1, device_id=peer, device_id_type=MESH_ID)
    peers = len(peers_always)
    for present, peer in sides:
        @pl.when(present)
        def _():
            pl.semaphore_signal(barrier, 1, device_id=peer, device_id_type=MESH_ID)

        peers = peers + present.astype(jnp.int32)
    pl.semaphore_wait(barrier, peers)


def exchange_kernel(groups, own_ref, pos_ref, own_bins_ref, near_bins_ref, row_key_ref,
                    window_key_ref, grad_ref, partner_win, pos_win, own_rows, partial, held,
                    local_sem, sec_send, sec_recv, fwd_send, fwd_recv, halo_send, halo_recv,
                    part_sems):
    rows = own_ref.shape[0]
    piece = rows // PIECES
    sec, wide, grp, has_left, has_right, left_id, right_id = place_of(groups)
    partner_id = (1 - sec, wide, grp)
    me = wide * groups + grp
    left_cross = has_left & ((me - 1) // groups // Y_CHIPS != wide // Y_CHIPS)
    right_cross = has_right & ((me + 1) // groups // Y_CHIPS != wide // Y_CHIPS)
    cross = (left_cross, right_cross)
    across_id = tuple((1 - sec,) + tuple(peer[1:]) for peer in (left_id, right_id))

    pos_win[:, pl.ds(rows, rows)] = pos_ref[...]
    own_copy = pltpu.make_async_copy(own_ref, own_rows, local_sem.at[3])
    own_copy.start()
    win = 3 * rows
    empty = jnp.full((1, rows), -jnp.inf, jnp.float32)
    held[0, :, pl.ds(2 * rows, rows)] = empty
    held[1, :, pl.ds(0, rows)] = empty

    @pl.when(jnp.logical_not(has_left))
    def _():
        held[0, :, pl.ds(0, 2 * rows)] = jnp.full((1, 2 * rows), -jnp.inf, jnp.float32)

    @pl.when(jnp.logical_not(has_right))
    def _():
        held[1, :, pl.ds(rows, 2 * rows)] = jnp.full((1, 2 * rows), -jnp.inf, jnp.float32)

    for d, arrived in ((0, has_right), (1, has_left)):
        @pl.when(jnp.logical_not(arrived))
        def _():
            place = pl.ds((1 - d) * 2 * rows, rows)
            partner_win[place, :] = jnp.zeros((rows, partner_win.shape[1]), partner_win.dtype)
            pos_win[:, pl.ds((1 - d) * 2 * rows, rows)] = jnp.zeros(pos_ref.shape, jnp.int32)

    greet((partner_id,), ((has_left, left_id), (has_right, right_id),
                          (left_cross, across_id[0]), (right_cross, across_id[1])))

    def sec_copy(q):
        return pltpu.make_async_remote_copy(
            src_ref=own_ref.at[pl.ds(q * piece, piece)],
            dst_ref=partner_win.at[pl.ds(rows + q * piece, piece)],
            send_sem=sec_send.at[q], recv_sem=sec_recv.at[q],
            device_id=partner_id, device_id_type=MESH_ID)

    def pos_copy(d):
        return pltpu.make_async_remote_copy(
            src_ref=pos_ref,
            dst_ref=pos_win.at[:, pl.ds((1 - d) * 2 * rows, rows)],
            send_sem=halo_send.at[d], recv_sem=halo_recv.at[d],
            device_id=left_id if d == 0 else right_id, device_id_type=MESH_ID)

    def fwd_copy(d, q):
        return pltpu.make_async_remote_copy(
            src_ref=partner_win.at[pl.ds(rows + q * piece, piece)],
            dst_ref=partner_win.at[pl.ds((1 - d) * 2 * rows + q * piece, piece)],
            send_sem=fwd_send.at[d, q], recv_sem=fwd_recv.at[d, q],
            device_id=left_id if d == 0 else right_id, device_id_type=MESH_ID)

    def cross_copy(d, q):
        return pltpu.make_async_remote_copy(
            src_ref=own_ref.at[pl.ds(q * piece, piece)],
            dst_ref=partner_win.at[pl.ds((1 - d) * 2 * rows + q * piece, piece)],
            send_sem=fwd_send.at[d, q], recv_sem=fwd_recv.at[d, q],
            device_id=across_id[d], device_id_type=MESH_ID)

    sides = ((0, has_left), (1, has_right))
    for d, present in sides:
        @pl.when(present)
        def _():
            pos_copy(d).start()

        @pl.when(cross[d])
        def _():
            for q in range(SPLIT):
                cross_copy(d, q).start()

    for q in range(IN_FLIGHT):
        sec_copy(q).start()
    for q in range(PIECES):
        sec_copy(q).wait_send()
        if q + IN_FLIGHT < PIECES:
            sec_copy(q + IN_FLIGHT).start()
        sec_copy(q).wait_recv()
        for d, present in sides:
            direct = cross[d] if q < SPLIT else False
            @pl.when(present & jnp.logical_not(direct))
            def _():
                fwd_copy(d, q).start()

    for d, present in sides:
        @pl.when(present)
        def _():
            pos_copy(d).wait_send()

        @pl.when(present & jnp.logical_not(cross[d]))
        def _():
            for q in range(SPLIT):
                fwd_copy(d, q).wait_send()

        @pl.when(present)
        def _():
            for q in range(SPLIT, PIECES):
                fwd_copy(d, q).wait_send()

        @pl.when(cross[d])
        def _():
            for q in range(SPLIT):
                cross_copy(d, q).wait_send()

        arrived = has_right if d == 0 else has_left

        @pl.when(arrived)
        def _():
            pos_copy(d).wait_recv()
            for q in range(PIECES):
                fwd_copy(d, q).wait_recv()

    own_copy.wait()
    scores = logit_scale * lax.dot_general(
        own_rows[...], partner_win[...], (((1,), (1,)), ((), ())),
        preferred_element_type=jnp.float32,
    )
    allowed = own_bins_ref[...] == near_bins_ref[...]
    own_total = masked_lse(scores, allowed, 1)
    partial[...] = masked_lse(scores, allowed, 0)

    def part_copy(d):
        return pltpu.make_async_remote_copy(
            src_ref=partial.at[:, pl.ds(d * rows, 2 * rows)],
            dst_ref=held.at[1 - d, :, pl.ds((1 - d) * rows, 2 * rows)],
            send_sem=part_sems.at[0, d], recv_sem=part_sems.at[1, d],
            device_id=left_id if d == 0 else right_id, device_id_type=MESH_ID)

    for d, present in sides:
        @pl.when(present)
        def _():
            part_copy(d).start()
    for d, present in sides:
        @pl.when(present)
        def _():
            part_copy(d).wait_send()

        arrived = has_right if d == 0 else has_left

        @pl.when(arrived)
        def _():
            part_copy(d).wait_recv()

    mine, left, right = partial[...], held[0], held[1]
    top = jnp.maximum(jnp.maximum(mine, left), right)
    top = jnp.where(top > -jnp.inf, top, 0.0)
    total = jnp.exp(mine - top) + jnp.exp(left - top) + jnp.exp(right - top)
    partner_total = jnp.log(total) + top

    col_key = jnp.where(sec == 0, window_key_ref[...], pos_win[...])
    hits = allowed & (row_key_ref[...] == col_key)
    weights = jnp.exp(scores - own_total) + jnp.exp(scores - partner_total)
    weights = jnp.where(allowed, weights, 0.0) - jnp.where(hits, 2.0, 0.0)
    grad = jnp.dot(weights.astype(jnp.bfloat16), partner_win[...], preferred_element_type=jnp.float32)
    grad_ref[...] = (logit_scale * grad).astype(grad_ref.dtype)


def exchange(own, positives, own_bins, near_bins, row_key, window_key, groups):
    rows, features = own.shape
    anywhere = pl.BlockSpec(memory_space=pl.ANY)
    vmem = pl.BlockSpec(memory_space=pltpu.VMEM)
    return pl.pallas_call(
        functools.partial(exchange_kernel, groups),
        out_shape=jax.ShapeDtypeStruct((rows, features), own.dtype),
        in_specs=[anywhere] + [vmem] * 5,
        out_specs=vmem,
        scratch_shapes=[
            pltpu.VMEM((3 * rows, features), own.dtype),
            pltpu.VMEM((1, 3 * rows), jnp.int32),
            pltpu.VMEM((rows, features), own.dtype),
            pltpu.VMEM((1, 3 * rows), jnp.float32),
            pltpu.VMEM((2, 1, 3 * rows), jnp.float32),
            pltpu.SemaphoreType.DMA((4,)),
            pltpu.SemaphoreType.DMA((PIECES,)),
            pltpu.SemaphoreType.DMA((PIECES,)),
            pltpu.SemaphoreType.DMA((2, PIECES)),
            pltpu.SemaphoreType.DMA((2, PIECES)),
            pltpu.SemaphoreType.DMA((2,)),
            pltpu.SemaphoreType.DMA((2,)),
            pltpu.SemaphoreType.DMA((2, 2)),
        ],
        compiler_params=pltpu.CompilerParams(
            collective_id=0, has_side_effects=True, vmem_limit_bytes=48 * 1024 * 1024
        ),
    )(own, positives[None, :], own_bins, near_bins, row_key, window_key)


def masked_lse(scores, allowed, axis):
    top = jnp.max(jnp.where(allowed, scores, -jnp.inf), axis=axis, keepdims=True)
    top = jnp.where(top > -jnp.inf, top, 0.0)
    total = jnp.sum(jnp.where(allowed, jnp.exp(scores - top), 0.0), axis=axis, keepdims=True)
    return jnp.log(total) + top


def local(embeddings, bin_ids, positives):
    own = embeddings[0]
    row_count, features = own.shape
    blocks = row_count // BLOCK
    groups = lax.axis_size("grp")
    me = lax.axis_index(ROWS)
    first_row = me * row_count
    spectral = lax.axis_index("sec") == 0

    win = 3 * row_count

    padded = jnp.pad(bin_ids, blocks, constant_values=-1)
    near_bins = jnp.repeat(lax.dynamic_slice_in_dim(padded, me * blocks, 3 * blocks, 0), BLOCK)
    own_bins = jnp.repeat(lax.dynamic_slice_in_dim(bin_ids, me * blocks, blocks, 0), BLOCK)
    own_bins = own_bins[:, None]
    near_bins = near_bins[None, :]
    window_index = first_row - row_count + jnp.arange(win, dtype=jnp.int32)
    own_index = first_row + jnp.arange(row_count, dtype=jnp.int32)
    row_key = jnp.where(spectral, positives, own_index)[:, None]
    grad = exchange(own, positives, own_bins, near_bins, row_key, window_index[None, :], groups)
    return grad[None]


def solution(mesh):
    in_specs = (P("sec", ROWS, None), P(), P(ROWS))
    out_specs = P("sec", ROWS, None)
    return jax.shard_map(local, mesh=mesh, in_specs=in_specs, out_specs=out_specs, check_vma=False)
```

```python
import functools

import jax
import jax.numpy as jnp
from jax import lax
from jax.experimental import pallas as pl
from jax.experimental.pallas import tpu as pltpu
from jax.sharding import PartitionSpec as P

BLOCK = 256
logit_scale = 0.125
ROWS = ("wide", "grp")


MESH_ID = pl.DeviceIdType.MESH
PIECES = 8
IN_FLIGHT = 2
Y_CHIPS = 8


def place_of(groups):
    sec = lax.axis_index("sec")
    wide = lax.axis_index("wide")
    grp = lax.axis_index("grp")
    count = lax.axis_size("wide") * groups
    me = wide * groups + grp
    left = jnp.maximum(me - 1, 0)
    right = jnp.minimum(me + 1, count - 1)
    left_id = (sec, left // groups, left % groups)
    right_id = (sec, right // groups, right % groups)
    return sec, wide, grp, me > 0, me < count - 1, left_id, right_id


def greet(peers_always, sides):
    barrier = pltpu.get_barrier_semaphore()
    for peer in peers_always:
        pl.semaphore_signal(barrier, 1, device_id=peer, device_id_type=MESH_ID)
    peers = len(peers_always)
    for present, peer in sides:
        @pl.when(present)
        def _():
            pl.semaphore_signal(barrier, 1, device_id=peer, device_id_type=MESH_ID)

        peers = peers + present.astype(jnp.int32)
    pl.semaphore_wait(barrier, peers)


def exchange_kernel(groups, own_ref, pos_ref, own_bins_ref, near_bins_ref, row_key_ref,
                    window_key_ref, grad_ref, partner_win, pos_win, own_rows, partial, held,
                    local_sem, sec_send, sec_recv, fwd_send, fwd_recv, halo_send, halo_recv,
                    part_sems):
    rows = own_ref.shape[0]
    piece = rows // PIECES
    sec, wide, grp, has_left, has_right, left_id, right_id = place_of(groups)
    partner_id = (1 - sec, wide, grp)
    me = wide * groups + grp
    left_cross = has_left & ((me - 1) // groups // Y_CHIPS != wide // Y_CHIPS)
    right_cross = has_right & ((me + 1) // groups // Y_CHIPS != wide // Y_CHIPS)
    cross = (left_cross, right_cross)
    across_id = tuple((1 - sec,) + tuple(peer[1:]) for peer in (left_id, right_id))

    pos_win[:, pl.ds(rows, rows)] = pos_ref[...]
    own_copy = pltpu.make_async_copy(own_ref, own_rows, local_sem.at[3])
    own_copy.start()
    win = 3 * rows
    empty = jnp.full((1, rows), -jnp.inf, jnp.float32)
    held[0, :, pl.ds(2 * rows, rows)] = empty
    held[1, :, pl.ds(0, rows)] = empty

    @pl.when(jnp.logical_not(has_left))
    def _():
        held[0, :, pl.ds(0, 2 * rows)] = jnp.full((1, 2 * rows), -jnp.inf, jnp.float32)

    @pl.when(jnp.logical_not(has_right))
    def _():
        held[1, :, pl.ds(rows, 2 * rows)] = jnp.full((1, 2 * rows), -jnp.inf, jnp.float32)

    for d, arrived in ((0, has_right), (1, has_left)):
        @pl.when(jnp.logical_not(arrived))
        def _():
            place = pl.ds((1 - d) * 2 * rows, rows)
            partner_win[place, :] = jnp.zeros((rows, partner_win.shape[1]), partner_win.dtype)
            pos_win[:, pl.ds((1 - d) * 2 * rows, rows)] = jnp.zeros(pos_ref.shape, jnp.int32)

    greet((partner_id,), ((has_left, left_id), (has_right, right_id),
                          (left_cross, across_id[0]), (right_cross, across_id[1])))

    def sec_copy(q):
        return pltpu.make_async_remote_copy(
            src_ref=own_ref.at[pl.ds(q * piece, piece)],
            dst_ref=partner_win.at[pl.ds(rows + q * piece, piece)],
            send_sem=sec_send.at[q], recv_sem=sec_recv.at[q],
            device_id=partner_id, device_id_type=MESH_ID)

    def pos_copy(d):
        return pltpu.make_async_remote_copy(
            src_ref=pos_ref,
            dst_ref=pos_win.at[:, pl.ds((1 - d) * 2 * rows, rows)],
            send_sem=halo_send.at[d], recv_sem=halo_recv.at[d],
            device_id=left_id if d == 0 else right_id, device_id_type=MESH_ID)

    def fwd_copy(d, q):
        return pltpu.make_async_remote_copy(
            src_ref=partner_win.at[pl.ds(rows + q * piece, piece)],
            dst_ref=partner_win.at[pl.ds((1 - d) * 2 * rows + q * piece, piece)],
            send_sem=fwd_send.at[d, q], recv_sem=fwd_recv.at[d, q],
            device_id=left_id if d == 0 else right_id, device_id_type=MESH_ID)

    def cross_copy(d, q):
        return pltpu.make_async_remote_copy(
            src_ref=own_ref.at[pl.ds(q * piece, piece)],
            dst_ref=partner_win.at[pl.ds((1 - d) * 2 * rows + q * piece, piece)],
            send_sem=fwd_send.at[d, q], recv_sem=fwd_recv.at[d, q],
            device_id=across_id[d], device_id_type=MESH_ID)

    sides = ((0, has_left), (1, has_right))
    for d, present in sides:
        @pl.when(present)
        def _():
            pos_copy(d).start()


    def send_piece(q):
        sec_copy(q).start()
        for d in range(2):
            @pl.when(cross[d])
            def _():
                cross_copy(d, q).start()

    for q in range(IN_FLIGHT):
        send_piece(q)
    for q in range(PIECES):
        sec_copy(q).wait_send()
        if q + IN_FLIGHT < PIECES:
            send_piece(q + IN_FLIGHT)
        sec_copy(q).wait_recv()
        for d, present in sides:
            @pl.when(present & jnp.logical_not(cross[d]))
            def _():
                fwd_copy(d, q).start()

    for d, present in sides:
        @pl.when(present)
        def _():
            pos_copy(d).wait_send()

        @pl.when(present & jnp.logical_not(cross[d]))
        def _():
            for q in range(PIECES):
                fwd_copy(d, q).wait_send()

        @pl.when(cross[d])
        def _():
            for q in range(PIECES):
                cross_copy(d, q).wait_send()

        arrived = has_right if d == 0 else has_left

        @pl.when(arrived)
        def _():
            pos_copy(d).wait_recv()
            for q in range(PIECES):
                fwd_copy(d, q).wait_recv()

    own_copy.wait()
    scores = logit_scale * lax.dot_general(
        own_rows[...], partner_win[...], (((1,), (1,)), ((), ())),
        preferred_element_type=jnp.float32,
    )
    allowed = own_bins_ref[...] == near_bins_ref[...]
    own_total = masked_lse(scores, allowed, 1)
    partial[...] = masked_lse(scores, allowed, 0)

    def part_copy(d):
        return pltpu.make_async_remote_copy(
            src_ref=partial.at[:, pl.ds(d * rows, 2 * rows)],
            dst_ref=held.at[1 - d, :, pl.ds((1 - d) * rows, 2 * rows)],
            send_sem=part_sems.at[0, d], recv_sem=part_sems.at[1, d],
            device_id=left_id if d == 0 else right_id, device_id_type=MESH_ID)

    for d, present in sides:
        @pl.when(present)
        def _():
            part_copy(d).start()
    for d, present in sides:
        @pl.when(present)
        def _():
            part_copy(d).wait_send()

        arrived = has_right if d == 0 else has_left

        @pl.when(arrived)
        def _():
            part_copy(d).wait_recv()

    mine, left, right = partial[...], held[0], held[1]
    top = jnp.maximum(jnp.maximum(mine, left), right)
    top = jnp.where(top > -jnp.inf, top, 0.0)
    total = jnp.exp(mine - top) + jnp.exp(left - top) + jnp.exp(right - top)
    partner_total = jnp.log(total) + top

    col_key = jnp.where(sec == 0, window_key_ref[...], pos_win[...])
    hits = allowed & (row_key_ref[...] == col_key)
    weights = jnp.exp(scores - own_total) + jnp.exp(scores - partner_total)
    weights = jnp.where(allowed, weights, 0.0) - jnp.where(hits, 2.0, 0.0)
    grad = jnp.dot(weights.astype(jnp.bfloat16), partner_win[...], preferred_element_type=jnp.float32)
    grad_ref[...] = (logit_scale * grad).astype(grad_ref.dtype)


def exchange(own, positives, own_bins, near_bins, row_key, window_key, groups):
    rows, features = own.shape
    anywhere = pl.BlockSpec(memory_space=pl.ANY)
    vmem = pl.BlockSpec(memory_space=pltpu.VMEM)
    return pl.pallas_call(
        functools.partial(exchange_kernel, groups),
        out_shape=jax.ShapeDtypeStruct((rows, features), own.dtype),
        in_specs=[anywhere] + [vmem] * 5,
        out_specs=vmem,
        scratch_shapes=[
            pltpu.VMEM((3 * rows, features), own.dtype),
            pltpu.VMEM((1, 3 * rows), jnp.int32),
            pltpu.VMEM((rows, features), own.dtype),
            pltpu.VMEM((1, 3 * rows), jnp.float32),
            pltpu.VMEM((2, 1, 3 * rows), jnp.float32),
            pltpu.SemaphoreType.DMA((4,)),
            pltpu.SemaphoreType.DMA((PIECES,)),
            pltpu.SemaphoreType.DMA((PIECES,)),
            pltpu.SemaphoreType.DMA((2, PIECES)),
            pltpu.SemaphoreType.DMA((2, PIECES)),
            pltpu.SemaphoreType.DMA((2,)),
            pltpu.SemaphoreType.DMA((2,)),
            pltpu.SemaphoreType.DMA((2, 2)),
        ],
        compiler_params=pltpu.CompilerParams(
            collective_id=0, has_side_effects=True, vmem_limit_bytes=48 * 1024 * 1024
        ),
    )(own, positives[None, :], own_bins, near_bins, row_key, window_key)


def masked_lse(scores, allowed, axis):
    top = jnp.max(jnp.where(allowed, scores, -jnp.inf), axis=axis, keepdims=True)
    top = jnp.where(top > -jnp.inf, top, 0.0)
    total = jnp.sum(jnp.where(allowed, jnp.exp(scores - top), 0.0), axis=axis, keepdims=True)
    return jnp.log(total) + top


def local(embeddings, bin_ids, positives):
    own = embeddings[0]
    row_count, features = own.shape
    blocks = row_count // BLOCK
    groups = lax.axis_size("grp")
    me = lax.axis_index(ROWS)
    first_row = me * row_count
    spectral = lax.axis_index("sec") == 0

    win = 3 * row_count

    padded = jnp.pad(bin_ids, blocks, constant_values=-1)
    near_bins = jnp.repeat(lax.dynamic_slice_in_dim(padded, me * blocks, 3 * blocks, 0), BLOCK)
    own_bins = jnp.repeat(lax.dynamic_slice_in_dim(bin_ids, me * blocks, blocks, 0), BLOCK)
    own_bins = own_bins[:, None]
    near_bins = near_bins[None, :]
    window_index = first_row - row_count + jnp.arange(win, dtype=jnp.int32)
    own_index = first_row + jnp.arange(row_count, dtype=jnp.int32)
    row_key = jnp.where(spectral, positives, own_index)[:, None]
    grad = exchange(own, positives, own_bins, near_bins, row_key, window_index[None, :], groups)
    return grad[None]


def solution(mesh):
    in_specs = (P("sec", ROWS, None), P(), P(ROWS))
    out_specs = P("sec", ROWS, None)
    return jax.shard_map(local, mesh=mesh, in_specs=in_specs, out_specs=out_specs, check_vma=False)
```

```python
import functools

import jax
import jax.numpy as jnp
from jax import lax
from jax.experimental import pallas as pl
from jax.experimental.pallas import tpu as pltpu
from jax.sharding import PartitionSpec as P

BLOCK = 256
logit_scale = 0.125
ROWS = ("wide", "grp")


MESH_ID = pl.DeviceIdType.MESH
PIECES = 8
IN_FLIGHT = 2
Y_CHIPS = 8


def place_of(groups):
    sec = lax.axis_index("sec")
    wide = lax.axis_index("wide")
    grp = lax.axis_index("grp")
    count = lax.axis_size("wide") * groups
    me = wide * groups + grp
    left = jnp.maximum(me - 1, 0)
    right = jnp.minimum(me + 1, count - 1)
    left_id = (sec, left // groups, left % groups)
    right_id = (sec, right // groups, right % groups)
    return sec, wide, grp, me > 0, me < count - 1, left_id, right_id


def greet(peers_always, sides):
    barrier = pltpu.get_barrier_semaphore()
    for peer in peers_always:
        pl.semaphore_signal(barrier, 1, device_id=peer, device_id_type=MESH_ID)
    peers = len(peers_always)
    for present, peer in sides:
        @pl.when(present)
        def _():
            pl.semaphore_signal(barrier, 1, device_id=peer, device_id_type=MESH_ID)

        peers = peers + present.astype(jnp.int32)
    pl.semaphore_wait(barrier, peers)


def exchange_kernel(groups, own_ref, pos_ref, own_bins_ref, near_bins_ref, row_key_ref,
                    window_key_ref, grad_ref, partner_win, pos_win, own_rows, partial, held,
                    local_sem, sec_send, sec_recv, fwd_send, fwd_recv, halo_send, halo_recv,
                    part_sems):
    rows = own_ref.shape[0]
    piece = rows // PIECES
    sec, wide, grp, has_left, has_right, left_id, right_id = place_of(groups)
    partner_id = (1 - sec, wide, grp)
    me = wide * groups + grp
    left_cross = has_left & ((me - 1) // groups // Y_CHIPS != wide // Y_CHIPS)
    right_cross = has_right & ((me + 1) // groups // Y_CHIPS != wide // Y_CHIPS)
    cross = (left_cross, right_cross)
    across_id = tuple((1 - sec,) + tuple(peer[1:]) for peer in (left_id, right_id))

    pos_win[:, pl.ds(rows, rows)] = pos_ref[...]
    own_copy = pltpu.make_async_copy(own_ref, own_rows, local_sem.at[3])
    own_copy.start()
    win = 3 * rows
    empty = jnp.full((1, rows), -jnp.inf, jnp.float32)
    held[0, :, pl.ds(2 * rows, rows)] = empty
    held[1, :, pl.ds(0, rows)] = empty

    @pl.when(jnp.logical_not(has_left))
    def _():
        held[0, :, pl.ds(0, 2 * rows)] = jnp.full((1, 2 * rows), -jnp.inf, jnp.float32)

    @pl.when(jnp.logical_not(has_right))
    def _():
        held[1, :, pl.ds(rows, 2 * rows)] = jnp.full((1, 2 * rows), -jnp.inf, jnp.float32)

    for d, arrived in ((0, has_right), (1, has_left)):
        @pl.when(jnp.logical_not(arrived))
        def _():
            place = pl.ds((1 - d) * 2 * rows, rows)
            partner_win[place, :] = jnp.zeros((rows, partner_win.shape[1]), partner_win.dtype)
            pos_win[:, pl.ds((1 - d) * 2 * rows, rows)] = jnp.zeros(pos_ref.shape, jnp.int32)

    greet((partner_id,), ((has_left, left_id), (has_right, right_id),
                          (left_cross, across_id[0]), (right_cross, across_id[1])))

    def sec_copy(q):
        return pltpu.make_async_remote_copy(
            src_ref=own_ref.at[pl.ds(q * piece, piece)],
            dst_ref=partner_win.at[pl.ds(rows + q * piece, piece)],
            send_sem=sec_send.at[q], recv_sem=sec_recv.at[q],
            device_id=partner_id, device_id_type=MESH_ID)

    def pos_copy(d):
        return pltpu.make_async_remote_copy(
            src_ref=pos_ref,
            dst_ref=pos_win.at[:, pl.ds((1 - d) * 2 * rows, rows)],
            send_sem=halo_send.at[d], recv_sem=halo_recv.at[d],
            device_id=left_id if d == 0 else right_id, device_id_type=MESH_ID)

    def fwd_copy(d, q):
        return pltpu.make_async_remote_copy(
            src_ref=partner_win.at[pl.ds(rows + q * piece, piece)],
            dst_ref=partner_win.at[pl.ds((1 - d) * 2 * rows + q * piece, piece)],
            send_sem=fwd_send.at[d, q], recv_sem=fwd_recv.at[d, q],
            device_id=left_id if d == 0 else right_id, device_id_type=MESH_ID)

    def cross_copy(d, q):
        return pltpu.make_async_remote_copy(
            src_ref=own_ref.at[pl.ds(q * piece, piece)],
            dst_ref=partner_win.at[pl.ds((1 - d) * 2 * rows + q * piece, piece)],
            send_sem=fwd_send.at[d, q], recv_sem=fwd_recv.at[d, q],
            device_id=across_id[d], device_id_type=MESH_ID)

    sides = ((0, has_left), (1, has_right))
    for d, present in sides:
        @pl.when(present)
        def _():
            pos_copy(d).start()

        @pl.when(cross[d])
        def _():
            for q in range(PIECES):
                cross_copy(d, q).start()

    for q in range(IN_FLIGHT):
        sec_copy(q).start()
    for q in range(PIECES):
        sec_copy(q).wait_send()
        if q + IN_FLIGHT < PIECES:
            sec_copy(q + IN_FLIGHT).start()
        sec_copy(q).wait_recv()
        for d, present in sides:
            @pl.when(present & jnp.logical_not(cross[d]))
            def _():
                fwd_copy(d, q).start()

    own_copy.wait()
    own_block = own_rows[...]

    def block_scores(k):
        scores = logit_scale * lax.dot_general(
            own_block, partner_win[pl.ds(k * rows, rows), :], (((1,), (1,)), ((), ())),
            preferred_element_type=jnp.float32,
        )
        return scores, own_bins_ref[...] == near_bins_ref[:, pl.ds(k * rows, rows)]

    def block_totals(k):
        scores, allowed = block_scores(k)
        partial[:, pl.ds(k * rows, rows)] = masked_lse(scores, allowed, 0)
        return scores, allowed, masked_lse(scores, allowed, 1)

    centre = block_totals(1)

    for d, present in sides:
        @pl.when(present)
        def _():
            pos_copy(d).wait_send()

        @pl.when(present & jnp.logical_not(cross[d]))
        def _():
            for q in range(PIECES):
                fwd_copy(d, q).wait_send()

        @pl.when(cross[d])
        def _():
            for q in range(PIECES):
                cross_copy(d, q).wait_send()

        arrived = has_right if d == 0 else has_left

        @pl.when(arrived)
        def _():
            pos_copy(d).wait_recv()
            for q in range(PIECES):
                fwd_copy(d, q).wait_recv()

    blocks = (block_totals(0), centre, block_totals(2))
    row_parts = [b[2] for b in blocks]
    top = jnp.maximum(jnp.maximum(row_parts[0], row_parts[1]), row_parts[2])
    top = jnp.where(top > -jnp.inf, top, 0.0)
    own_total = jnp.log(sum(jnp.exp(p - top) for p in row_parts)) + top

    def part_copy(d):
        return pltpu.make_async_remote_copy(
            src_ref=partial.at[:, pl.ds(d * rows, 2 * rows)],
            dst_ref=held.at[1 - d, :, pl.ds((1 - d) * rows, 2 * rows)],
            send_sem=part_sems.at[0, d], recv_sem=part_sems.at[1, d],
            device_id=left_id if d == 0 else right_id, device_id_type=MESH_ID)

    for d, present in sides:
        @pl.when(present)
        def _():
            part_copy(d).start()
    for d, present in sides:
        @pl.when(present)
        def _():
            part_copy(d).wait_send()

        arrived = has_right if d == 0 else has_left

        @pl.when(arrived)
        def _():
            part_copy(d).wait_recv()

    mine, left, right = partial[...], held[0], held[1]
    top = jnp.maximum(jnp.maximum(mine, left), right)
    top = jnp.where(top > -jnp.inf, top, 0.0)
    total = jnp.exp(mine - top) + jnp.exp(left - top) + jnp.exp(right - top)
    partner_total = jnp.log(total) + top

    col_key = jnp.where(sec == 0, window_key_ref[...], pos_win[...])
    grad = None
    for k, (scores, allowed, _) in enumerate(blocks):
        columns = slice(k * rows, (k + 1) * rows)
        hits = allowed & (row_key_ref[...] == col_key[:, columns])
        weights = jnp.exp(scores - own_total) + jnp.exp(scores - partner_total[:, columns])
        weights = jnp.where(allowed, weights, 0.0) - jnp.where(hits, 2.0, 0.0)
        term = jnp.dot(weights.astype(jnp.bfloat16), partner_win[pl.ds(k * rows, rows), :],
                       preferred_element_type=jnp.float32)
        grad = term if grad is None else grad + term
    grad_ref[...] = (logit_scale * grad).astype(grad_ref.dtype)


def exchange(own, positives, own_bins, near_bins, row_key, window_key, groups):
    rows, features = own.shape
    anywhere = pl.BlockSpec(memory_space=pl.ANY)
    vmem = pl.BlockSpec(memory_space=pltpu.VMEM)
    return pl.pallas_call(
        functools.partial(exchange_kernel, groups),
        out_shape=jax.ShapeDtypeStruct((rows, features), own.dtype),
        in_specs=[anywhere] + [vmem] * 5,
        out_specs=vmem,
        scratch_shapes=[
            pltpu.VMEM((3 * rows, features), own.dtype),
            pltpu.VMEM((1, 3 * rows), jnp.int32),
            pltpu.VMEM((rows, features), own.dtype),
            pltpu.VMEM((1, 3 * rows), jnp.float32),
            pltpu.VMEM((2, 1, 3 * rows), jnp.float32),
            pltpu.SemaphoreType.DMA((4,)),
            pltpu.SemaphoreType.DMA((PIECES,)),
            pltpu.SemaphoreType.DMA((PIECES,)),
            pltpu.SemaphoreType.DMA((2, PIECES)),
            pltpu.SemaphoreType.DMA((2, PIECES)),
            pltpu.SemaphoreType.DMA((2,)),
            pltpu.SemaphoreType.DMA((2,)),
            pltpu.SemaphoreType.DMA((2, 2)),
        ],
        compiler_params=pltpu.CompilerParams(
            collective_id=0, has_side_effects=True, vmem_limit_bytes=48 * 1024 * 1024
        ),
    )(own, positives[None, :], own_bins, near_bins, row_key, window_key)


def masked_lse(scores, allowed, axis):
    top = jnp.max(jnp.where(allowed, scores, -jnp.inf), axis=axis, keepdims=True)
    top = jnp.where(top > -jnp.inf, top, 0.0)
    total = jnp.sum(jnp.where(allowed, jnp.exp(scores - top), 0.0), axis=axis, keepdims=True)
    return jnp.log(total) + top


def local(embeddings, bin_ids, positives):
    own = embeddings[0]
    row_count, features = own.shape
    blocks = row_count // BLOCK
    groups = lax.axis_size("grp")
    me = lax.axis_index(ROWS)
    first_row = me * row_count
    spectral = lax.axis_index("sec") == 0

    win = 3 * row_count

    padded = jnp.pad(bin_ids, blocks, constant_values=-1)
    near_bins = jnp.repeat(lax.dynamic_slice_in_dim(padded, me * blocks, 3 * blocks, 0), BLOCK)
    own_bins = jnp.repeat(lax.dynamic_slice_in_dim(bin_ids, me * blocks, blocks, 0), BLOCK)
    own_bins = own_bins[:, None]
    near_bins = near_bins[None, :]
    window_index = first_row - row_count + jnp.arange(win, dtype=jnp.int32)
    own_index = first_row + jnp.arange(row_count, dtype=jnp.int32)
    row_key = jnp.where(spectral, positives, own_index)[:, None]
    grad = exchange(own, positives, own_bins, near_bins, row_key, window_index[None, :], groups)
    return grad[None]


def solution(mesh):
    in_specs = (P("sec", ROWS, None), P(), P(ROWS))
    out_specs = P("sec", ROWS, None)
    return jax.shard_map(local, mesh=mesh, in_specs=in_specs, out_specs=out_specs, check_vma=False)
```

```python
import functools

import jax
import jax.numpy as jnp
from jax import lax
from jax.experimental import pallas as pl
from jax.experimental.pallas import tpu as pltpu
from jax.sharding import PartitionSpec as P

BLOCK = 256
logit_scale = 0.125
ROWS = ("wide", "grp")


MESH_ID = pl.DeviceIdType.MESH
PIECES = 8
IN_FLIGHT = 2
Y_CHIPS = 8


def place_of(groups):
    sec = lax.axis_index("sec")
    wide = lax.axis_index("wide")
    grp = lax.axis_index("grp")
    count = lax.axis_size("wide") * groups
    me = wide * groups + grp
    left = jnp.maximum(me - 1, 0)
    right = jnp.minimum(me + 1, count - 1)
    left_id = (sec, left // groups, left % groups)
    right_id = (sec, right // groups, right % groups)
    return sec, wide, grp, me > 0, me < count - 1, left_id, right_id


def greet(peers_always, sides):
    barrier = pltpu.get_barrier_semaphore()
    for peer in peers_always:
        pl.semaphore_signal(barrier, 1, device_id=peer, device_id_type=MESH_ID)
    peers = len(peers_always)
    for present, peer in sides:
        @pl.when(present)
        def _():
            pl.semaphore_signal(barrier, 1, device_id=peer, device_id_type=MESH_ID)

        peers = peers + present.astype(jnp.int32)
    pl.semaphore_wait(barrier, peers)


def exchange_kernel(groups, own_ref, pos_ref, own_bins_ref, near_bins_ref, row_key_ref,
                    window_key_ref, grad_ref, partner_win, pos_win, own_rows, partial, held,
                    score_buf, row_buf, local_sem, sec_send, sec_recv, fwd_send, fwd_recv,
                    halo_send, halo_recv, part_sems):
    rows = own_ref.shape[0]
    piece = rows // PIECES
    sec, wide, grp, has_left, has_right, left_id, right_id = place_of(groups)
    partner_id = (1 - sec, wide, grp)
    me = wide * groups + grp
    left_cross = has_left & ((me - 1) // groups // Y_CHIPS != wide // Y_CHIPS)
    right_cross = has_right & ((me + 1) // groups // Y_CHIPS != wide // Y_CHIPS)
    cross = (left_cross, right_cross)
    across_id = tuple((1 - sec,) + tuple(peer[1:]) for peer in (left_id, right_id))

    pos_win[:, pl.ds(rows, rows)] = pos_ref[...]
    own_copy = pltpu.make_async_copy(own_ref, own_rows, local_sem.at[3])
    own_copy.start()
    win = 3 * rows
    empty = jnp.full((1, rows), -jnp.inf, jnp.float32)
    held[0, :, pl.ds(2 * rows, rows)] = empty
    held[1, :, pl.ds(0, rows)] = empty

    @pl.when(jnp.logical_not(has_left))
    def _():
        held[0, :, pl.ds(0, 2 * rows)] = jnp.full((1, 2 * rows), -jnp.inf, jnp.float32)

    @pl.when(jnp.logical_not(has_right))
    def _():
        held[1, :, pl.ds(rows, 2 * rows)] = jnp.full((1, 2 * rows), -jnp.inf, jnp.float32)

    for d, arrived in ((0, has_right), (1, has_left)):
        @pl.when(jnp.logical_not(arrived))
        def _():
            place = pl.ds((1 - d) * 2 * rows, rows)
            partner_win[place, :] = jnp.zeros((rows, partner_win.shape[1]), partner_win.dtype)
            pos_win[:, pl.ds((1 - d) * 2 * rows, rows)] = jnp.zeros(pos_ref.shape, jnp.int32)

    greet((partner_id,), ((has_left, left_id), (has_right, right_id),
                          (left_cross, across_id[0]), (right_cross, across_id[1])))

    def sec_copy(q):
        return pltpu.make_async_remote_copy(
            src_ref=own_ref.at[pl.ds(q * piece, piece)],
            dst_ref=partner_win.at[pl.ds(rows + q * piece, piece)],
            send_sem=sec_send.at[q], recv_sem=sec_recv.at[q],
            device_id=partner_id, device_id_type=MESH_ID)

    def pos_copy(d):
        return pltpu.make_async_remote_copy(
            src_ref=pos_ref,
            dst_ref=pos_win.at[:, pl.ds((1 - d) * 2 * rows, rows)],
            send_sem=halo_send.at[d], recv_sem=halo_recv.at[d],
            device_id=left_id if d == 0 else right_id, device_id_type=MESH_ID)

    def fwd_copy(d, q):
        return pltpu.make_async_remote_copy(
            src_ref=partner_win.at[pl.ds(rows + q * piece, piece)],
            dst_ref=partner_win.at[pl.ds((1 - d) * 2 * rows + q * piece, piece)],
            send_sem=fwd_send.at[d, q], recv_sem=fwd_recv.at[d, q],
            device_id=left_id if d == 0 else right_id, device_id_type=MESH_ID)

    def cross_copy(d, q):
        return pltpu.make_async_remote_copy(
            src_ref=own_ref.at[pl.ds(q * piece, piece)],
            dst_ref=partner_win.at[pl.ds((1 - d) * 2 * rows + q * piece, piece)],
            send_sem=fwd_send.at[d, q], recv_sem=fwd_recv.at[d, q],
            device_id=across_id[d], device_id_type=MESH_ID)

    sides = ((0, has_left), (1, has_right))
    for d, present in sides:
        @pl.when(present)
        def _():
            pos_copy(d).start()

        @pl.when(cross[d])
        def _():
            for q in range(PIECES):
                cross_copy(d, q).start()

    for q in range(IN_FLIGHT):
        sec_copy(q).start()
    for q in range(PIECES):
        sec_copy(q).wait_send()
        if q + IN_FLIGHT < PIECES:
            sec_copy(q + IN_FLIGHT).start()
        sec_copy(q).wait_recv()
        for d, present in sides:
            @pl.when(present & jnp.logical_not(cross[d]))
            def _():
                fwd_copy(d, q).start()

    own_copy.wait()
    own_block = own_rows[...]

    def block_scores(k):
        scores = logit_scale * lax.dot_general(
            own_block, partner_win[pl.ds(k * rows, rows), :], (((1,), (1,)), ((), ())),
            preferred_element_type=jnp.float32,
        )
        return scores, own_bins_ref[...] == near_bins_ref[:, pl.ds(k * rows, rows)]

    def block_totals(k):
        scores, allowed = block_scores(k)
        partial[:, pl.ds(k * rows, rows)] = masked_lse(scores, allowed, 0)
        score_buf[k] = scores
        row_buf[k] = masked_lse(scores, allowed, 1)

    block_totals(1)

    def halo_block(k):
        d = 1 if k == 0 else 0
        arrived = has_left if k == 0 else has_right

        @pl.when(arrived)
        def _():
            pos_copy(d).wait_recv()
            for q in range(PIECES):
                fwd_copy(d, q).wait_recv()

        block_totals(k)

    for first, second in ((2, 0), (0, 2)):
        @pl.when((grp == 0) == (first == 2))
        def _():
            halo_block(first)
            halo_block(second)

    for d, present in sides:
        @pl.when(present)
        def _():
            pos_copy(d).wait_send()

        @pl.when(present & jnp.logical_not(cross[d]))
        def _():
            for q in range(PIECES):
                fwd_copy(d, q).wait_send()

        @pl.when(cross[d])
        def _():
            for q in range(PIECES):
                cross_copy(d, q).wait_send()


    row_parts = [row_buf[k] for k in range(3)]
    top = jnp.maximum(jnp.maximum(row_parts[0], row_parts[1]), row_parts[2])
    top = jnp.where(top > -jnp.inf, top, 0.0)
    own_total = jnp.log(sum(jnp.exp(p - top) for p in row_parts)) + top

    def part_copy(d):
        return pltpu.make_async_remote_copy(
            src_ref=partial.at[:, pl.ds(d * rows, 2 * rows)],
            dst_ref=held.at[1 - d, :, pl.ds((1 - d) * rows, 2 * rows)],
            send_sem=part_sems.at[0, d], recv_sem=part_sems.at[1, d],
            device_id=left_id if d == 0 else right_id, device_id_type=MESH_ID)

    for d, present in sides:
        @pl.when(present)
        def _():
            part_copy(d).start()
    for d, present in sides:
        @pl.when(present)
        def _():
            part_copy(d).wait_send()

        arrived = has_right if d == 0 else has_left

        @pl.when(arrived)
        def _():
            part_copy(d).wait_recv()

    mine, left, right = partial[...], held[0], held[1]
    top = jnp.maximum(jnp.maximum(mine, left), right)
    top = jnp.where(top > -jnp.inf, top, 0.0)
    total = jnp.exp(mine - top) + jnp.exp(left - top) + jnp.exp(right - top)
    partner_total = jnp.log(total) + top

    col_key = jnp.where(sec == 0, window_key_ref[...], pos_win[...])
    grad = None
    for k in range(3):
        columns = slice(k * rows, (k + 1) * rows)
        scores = score_buf[k]
        allowed = own_bins_ref[...] == near_bins_ref[:, pl.ds(k * rows, rows)]
        hits = allowed & (row_key_ref[...] == col_key[:, columns])
        weights = jnp.exp(scores - own_total) + jnp.exp(scores - partner_total[:, columns])
        weights = jnp.where(allowed, weights, 0.0) - jnp.where(hits, 2.0, 0.0)
        term = jnp.dot(weights.astype(jnp.bfloat16), partner_win[pl.ds(k * rows, rows), :],
                       preferred_element_type=jnp.float32)
        grad = term if grad is None else grad + term
    grad_ref[...] = (logit_scale * grad).astype(grad_ref.dtype)


def exchange(own, positives, own_bins, near_bins, row_key, window_key, groups):
    rows, features = own.shape
    anywhere = pl.BlockSpec(memory_space=pl.ANY)
    vmem = pl.BlockSpec(memory_space=pltpu.VMEM)
    return pl.pallas_call(
        functools.partial(exchange_kernel, groups),
        out_shape=jax.ShapeDtypeStruct((rows, features), own.dtype),
        in_specs=[anywhere] + [vmem] * 5,
        out_specs=vmem,
        scratch_shapes=[
            pltpu.VMEM((3 * rows, features), own.dtype),
            pltpu.VMEM((1, 3 * rows), jnp.int32),
            pltpu.VMEM((rows, features), own.dtype),
            pltpu.VMEM((1, 3 * rows), jnp.float32),
            pltpu.VMEM((2, 1, 3 * rows), jnp.float32),
            pltpu.VMEM((3, rows, rows), jnp.float32),
            pltpu.VMEM((3, rows, 1), jnp.float32),
            pltpu.SemaphoreType.DMA((4,)),
            pltpu.SemaphoreType.DMA((PIECES,)),
            pltpu.SemaphoreType.DMA((PIECES,)),
            pltpu.SemaphoreType.DMA((2, PIECES)),
            pltpu.SemaphoreType.DMA((2, PIECES)),
            pltpu.SemaphoreType.DMA((2,)),
            pltpu.SemaphoreType.DMA((2,)),
            pltpu.SemaphoreType.DMA((2, 2)),
        ],
        compiler_params=pltpu.CompilerParams(
            collective_id=0, has_side_effects=True, vmem_limit_bytes=48 * 1024 * 1024
        ),
    )(own, positives[None, :], own_bins, near_bins, row_key, window_key)


def masked_lse(scores, allowed, axis):
    top = jnp.max(jnp.where(allowed, scores, -jnp.inf), axis=axis, keepdims=True)
    top = jnp.where(top > -jnp.inf, top, 0.0)
    total = jnp.sum(jnp.where(allowed, jnp.exp(scores - top), 0.0), axis=axis, keepdims=True)
    return jnp.log(total) + top


def local(embeddings, bin_ids, positives):
    own = embeddings[0]
    row_count, features = own.shape
    blocks = row_count // BLOCK
    groups = lax.axis_size("grp")
    me = lax.axis_index(ROWS)
    first_row = me * row_count
    spectral = lax.axis_index("sec") == 0

    win = 3 * row_count

    padded = jnp.pad(bin_ids, blocks, constant_values=-1)
    near_bins = jnp.repeat(lax.dynamic_slice_in_dim(padded, me * blocks, 3 * blocks, 0), BLOCK)
    own_bins = jnp.repeat(lax.dynamic_slice_in_dim(bin_ids, me * blocks, blocks, 0), BLOCK)
    own_bins = own_bins[:, None]
    near_bins = near_bins[None, :]
    window_index = first_row - row_count + jnp.arange(win, dtype=jnp.int32)
    own_index = first_row + jnp.arange(row_count, dtype=jnp.int32)
    row_key = jnp.where(spectral, positives, own_index)[:, None]
    grad = exchange(own, positives, own_bins, near_bins, row_key, window_index[None, :], groups)
    return grad[None]


def solution(mesh):
    in_specs = (P("sec", ROWS, None), P(), P(ROWS))
    out_specs = P("sec", ROWS, None)
    return jax.shard_map(local, mesh=mesh, in_specs=in_specs, out_specs=out_specs, check_vma=False)
```

```python
import functools

import jax
import jax.numpy as jnp
from jax import lax
from jax.experimental import pallas as pl
from jax.experimental.pallas import tpu as pltpu
from jax.sharding import PartitionSpec as P

BLOCK = 256
logit_scale = 0.125
ROWS = ("wide", "grp")


MESH_ID = pl.DeviceIdType.MESH
PIECES = 4
IN_FLIGHT = 2
Y_CHIPS = 8


def place_of(groups):
    sec = lax.axis_index("sec")
    wide = lax.axis_index("wide")
    grp = lax.axis_index("grp")
    count = lax.axis_size("wide") * groups
    me = wide * groups + grp
    left = jnp.maximum(me - 1, 0)
    right = jnp.minimum(me + 1, count - 1)
    left_id = (sec, left // groups, left % groups)
    right_id = (sec, right // groups, right % groups)
    return sec, wide, grp, me > 0, me < count - 1, left_id, right_id


def greet(peers_always, sides):
    barrier = pltpu.get_barrier_semaphore()
    for peer in peers_always:
        pl.semaphore_signal(barrier, 1, device_id=peer, device_id_type=MESH_ID)
    peers = len(peers_always)
    for present, peer in sides:
        @pl.when(present)
        def _():
            pl.semaphore_signal(barrier, 1, device_id=peer, device_id_type=MESH_ID)

        peers = peers + present.astype(jnp.int32)
    pl.semaphore_wait(barrier, peers)


def exchange_kernel(groups, own_ref, pos_ref, own_bins_ref, near_bins_ref, row_key_ref,
                    window_key_ref, grad_ref, partner_win, pos_win, own_rows, partial, held,
                    centre_buf, local_sem, sec_send, sec_recv, fwd_send, fwd_recv, halo_send,
                    halo_recv, part_sems):
    rows = own_ref.shape[0]
    piece = rows // PIECES
    sec, wide, grp, has_left, has_right, left_id, right_id = place_of(groups)
    partner_id = (1 - sec, wide, grp)
    me = wide * groups + grp
    left_cross = has_left & ((me - 1) // groups // Y_CHIPS != wide // Y_CHIPS)
    right_cross = has_right & ((me + 1) // groups // Y_CHIPS != wide // Y_CHIPS)
    cross = (left_cross, right_cross)
    across_id = tuple((1 - sec,) + tuple(peer[1:]) for peer in (left_id, right_id))

    pos_win[:, pl.ds(rows, rows)] = pos_ref[...]
    own_copy = pltpu.make_async_copy(own_ref, own_rows, local_sem.at[3])
    own_copy.start()
    win = 3 * rows
    empty = jnp.full((1, rows), -jnp.inf, jnp.float32)
    held[0, :, pl.ds(2 * rows, rows)] = empty
    held[1, :, pl.ds(0, rows)] = empty

    @pl.when(jnp.logical_not(has_left))
    def _():
        held[0, :, pl.ds(0, 2 * rows)] = jnp.full((1, 2 * rows), -jnp.inf, jnp.float32)

    @pl.when(jnp.logical_not(has_right))
    def _():
        held[1, :, pl.ds(rows, 2 * rows)] = jnp.full((1, 2 * rows), -jnp.inf, jnp.float32)

    for d, arrived in ((0, has_right), (1, has_left)):
        @pl.when(jnp.logical_not(arrived))
        def _():
            place = pl.ds((1 - d) * 2 * rows, rows)
            partner_win[place, :] = jnp.zeros((rows, partner_win.shape[1]), partner_win.dtype)
            pos_win[:, pl.ds((1 - d) * 2 * rows, rows)] = jnp.zeros(pos_ref.shape, jnp.int32)

    greet((partner_id,), ((has_left, left_id), (has_right, right_id),
                          (left_cross, across_id[0]), (right_cross, across_id[1])))

    def sec_copy(q):
        return pltpu.make_async_remote_copy(
            src_ref=own_ref.at[pl.ds(q * piece, piece)],
            dst_ref=partner_win.at[pl.ds(rows + q * piece, piece)],
            send_sem=sec_send.at[q], recv_sem=sec_recv.at[q],
            device_id=partner_id, device_id_type=MESH_ID)

    def pos_copy(d):
        return pltpu.make_async_remote_copy(
            src_ref=pos_ref,
            dst_ref=pos_win.at[:, pl.ds((1 - d) * 2 * rows, rows)],
            send_sem=halo_send.at[d], recv_sem=halo_recv.at[d],
            device_id=left_id if d == 0 else right_id, device_id_type=MESH_ID)

    def fwd_copy(d, q):
        return pltpu.make_async_remote_copy(
            src_ref=partner_win.at[pl.ds(rows + q * piece, piece)],
            dst_ref=partner_win.at[pl.ds((1 - d) * 2 * rows + q * piece, piece)],
            send_sem=fwd_send.at[d, q], recv_sem=fwd_recv.at[d, q],
            device_id=left_id if d == 0 else right_id, device_id_type=MESH_ID)

    def cross_copy(d, q):
        return pltpu.make_async_remote_copy(
            src_ref=own_ref.at[pl.ds(q * piece, piece)],
            dst_ref=partner_win.at[pl.ds((1 - d) * 2 * rows + q * piece, piece)],
            send_sem=fwd_send.at[d, q], recv_sem=fwd_recv.at[d, q],
            device_id=across_id[d], device_id_type=MESH_ID)

    sides = ((0, has_left), (1, has_right))
    for d, present in sides:
        @pl.when(present)
        def _():
            pos_copy(d).start()

        @pl.when(cross[d])
        def _():
            for q in range(PIECES):
                cross_copy(d, q).start()

    for q in range(IN_FLIGHT):
        sec_copy(q).start()
    for q in range(PIECES):
        sec_copy(q).wait_send()
        if q + IN_FLIGHT < PIECES:
            sec_copy(q + IN_FLIGHT).start()
        sec_copy(q).wait_recv()
        for d, present in sides:
            @pl.when(present & jnp.logical_not(cross[d]))
            def _():
                fwd_copy(d, q).start()
        if q == 0:
            own_copy.wait()
        centre_buf[:, pl.ds(q * piece, piece)] = logit_scale * lax.dot_general(
            own_rows[...], partner_win[pl.ds(rows + q * piece, piece), :],
            (((1,), (1,)), ((), ())), preferred_element_type=jnp.float32,
        )

    own_block = own_rows[...]

    def block_scores(k):
        scores = logit_scale * lax.dot_general(
            own_block, partner_win[pl.ds(k * rows, rows), :], (((1,), (1,)), ((), ())),
            preferred_element_type=jnp.float32,
        )
        return scores, own_bins_ref[...] == near_bins_ref[:, pl.ds(k * rows, rows)]

    def block_totals(k):
        if k == 1:
            scores = centre_buf[...]
            allowed = own_bins_ref[...] == near_bins_ref[:, pl.ds(rows, rows)]
        else:
            scores, allowed = block_scores(k)
        partial[:, pl.ds(k * rows, rows)] = masked_lse(scores, allowed, 0)
        return scores, allowed, masked_lse(scores, allowed, 1)

    centre = block_totals(1)

    for d, present in sides:
        @pl.when(present)
        def _():
            pos_copy(d).wait_send()

        @pl.when(present & jnp.logical_not(cross[d]))
        def _():
            for q in range(PIECES):
                fwd_copy(d, q).wait_send()

        @pl.when(cross[d])
        def _():
            for q in range(PIECES):
                cross_copy(d, q).wait_send()

        arrived = has_right if d == 0 else has_left

        @pl.when(arrived)
        def _():
            pos_copy(d).wait_recv()
            for q in range(PIECES):
                fwd_copy(d, q).wait_recv()

    blocks = (block_totals(0), centre, block_totals(2))
    row_parts = [b[2] for b in blocks]
    top = jnp.maximum(jnp.maximum(row_parts[0], row_parts[1]), row_parts[2])
    top = jnp.where(top > -jnp.inf, top, 0.0)
    own_total = jnp.log(sum(jnp.exp(p - top) for p in row_parts)) + top

    def part_copy(d):
        return pltpu.make_async_remote_copy(
            src_ref=partial.at[:, pl.ds(d * rows, 2 * rows)],
            dst_ref=held.at[1 - d, :, pl.ds((1 - d) * rows, 2 * rows)],
            send_sem=part_sems.at[0, d], recv_sem=part_sems.at[1, d],
            device_id=left_id if d == 0 else right_id, device_id_type=MESH_ID)

    for d, present in sides:
        @pl.when(present)
        def _():
            part_copy(d).start()
    for d, present in sides:
        @pl.when(present)
        def _():
            part_copy(d).wait_send()

        arrived = has_right if d == 0 else has_left

        @pl.when(arrived)
        def _():
            part_copy(d).wait_recv()

    mine, left, right = partial[...], held[0], held[1]
    top = jnp.maximum(jnp.maximum(mine, left), right)
    top = jnp.where(top > -jnp.inf, top, 0.0)
    total = jnp.exp(mine - top) + jnp.exp(left - top) + jnp.exp(right - top)
    partner_total = jnp.log(total) + top

    col_key = jnp.where(sec == 0, window_key_ref[...], pos_win[...])
    grad = None
    for k, (scores, allowed, _) in enumerate(blocks):
        columns = slice(k * rows, (k + 1) * rows)
        hits = allowed & (row_key_ref[...] == col_key[:, columns])
        weights = jnp.exp(scores - own_total) + jnp.exp(scores - partner_total[:, columns])
        weights = jnp.where(allowed, weights, 0.0) - jnp.where(hits, 2.0, 0.0)
        term = jnp.dot(weights.astype(jnp.bfloat16), partner_win[pl.ds(k * rows, rows), :],
                       preferred_element_type=jnp.float32)
        grad = term if grad is None else grad + term
    grad_ref[...] = (logit_scale * grad).astype(grad_ref.dtype)


def exchange(own, positives, own_bins, near_bins, row_key, window_key, groups):
    rows, features = own.shape
    anywhere = pl.BlockSpec(memory_space=pl.ANY)
    vmem = pl.BlockSpec(memory_space=pltpu.VMEM)
    return pl.pallas_call(
        functools.partial(exchange_kernel, groups),
        out_shape=jax.ShapeDtypeStruct((rows, features), own.dtype),
        in_specs=[anywhere] + [vmem] * 5,
        out_specs=vmem,
        scratch_shapes=[
            pltpu.VMEM((3 * rows, features), own.dtype),
            pltpu.VMEM((1, 3 * rows), jnp.int32),
            pltpu.VMEM((rows, features), own.dtype),
            pltpu.VMEM((1, 3 * rows), jnp.float32),
            pltpu.VMEM((2, 1, 3 * rows), jnp.float32),
            pltpu.VMEM((rows, rows), jnp.float32),
            pltpu.SemaphoreType.DMA((4,)),
            pltpu.SemaphoreType.DMA((PIECES,)),
            pltpu.SemaphoreType.DMA((PIECES,)),
            pltpu.SemaphoreType.DMA((2, PIECES)),
            pltpu.SemaphoreType.DMA((2, PIECES)),
            pltpu.SemaphoreType.DMA((2,)),
            pltpu.SemaphoreType.DMA((2,)),
            pltpu.SemaphoreType.DMA((2, 2)),
        ],
        compiler_params=pltpu.CompilerParams(
            collective_id=0, has_side_effects=True, vmem_limit_bytes=48 * 1024 * 1024
        ),
    )(own, positives[None, :], own_bins, near_bins, row_key, window_key)


def masked_lse(scores, allowed, axis):
    top = jnp.max(jnp.where(allowed, scores, -jnp.inf), axis=axis, keepdims=True)
    top = jnp.where(top > -jnp.inf, top, 0.0)
    total = jnp.sum(jnp.where(allowed, jnp.exp(scores - top), 0.0), axis=axis, keepdims=True)
    return jnp.log(total) + top


def local(embeddings, bin_ids, positives):
    own = embeddings[0]
    row_count, features = own.shape
    blocks = row_count // BLOCK
    groups = lax.axis_size("grp")
    me = lax.axis_index(ROWS)
    first_row = me * row_count
    spectral = lax.axis_index("sec") == 0

    win = 3 * row_count

    padded = jnp.pad(bin_ids, blocks, constant_values=-1)
    near_bins = jnp.repeat(lax.dynamic_slice_in_dim(padded, me * blocks, 3 * blocks, 0), BLOCK)
    own_bins = jnp.repeat(lax.dynamic_slice_in_dim(bin_ids, me * blocks, blocks, 0), BLOCK)
    own_bins = own_bins[:, None]
    near_bins = near_bins[None, :]
    window_index = first_row - row_count + jnp.arange(win, dtype=jnp.int32)
    own_index = first_row + jnp.arange(row_count, dtype=jnp.int32)
    row_key = jnp.where(spectral, positives, own_index)[:, None]
    grad = exchange(own, positives, own_bins, near_bins, row_key, window_index[None, :], groups)
    return grad[None]


def solution(mesh):
    in_specs = (P("sec", ROWS, None), P(), P(ROWS))
    out_specs = P("sec", ROWS, None)
    return jax.shard_map(local, mesh=mesh, in_specs=in_specs, out_specs=out_specs, check_vma=False)
```

```python
import functools

import jax
import jax.numpy as jnp
from jax import lax
from jax.experimental import pallas as pl
from jax.experimental.pallas import tpu as pltpu
from jax.sharding import PartitionSpec as P

BLOCK = 256
logit_scale = 0.125
ROWS = ("wide", "grp")


MESH_ID = pl.DeviceIdType.MESH
PIECES = 8
IN_FLIGHT = 2
Y_CHIPS = 8


def place_of(groups):
    sec = lax.axis_index("sec")
    wide = lax.axis_index("wide")
    grp = lax.axis_index("grp")
    count = lax.axis_size("wide") * groups
    me = wide * groups + grp
    left = jnp.maximum(me - 1, 0)
    right = jnp.minimum(me + 1, count - 1)
    left_id = (sec, left // groups, left % groups)
    right_id = (sec, right // groups, right % groups)
    return sec, wide, grp, me > 0, me < count - 1, left_id, right_id


def greet(peers_always, sides):
    barrier = pltpu.get_barrier_semaphore()
    for peer in peers_always:
        pl.semaphore_signal(barrier, 1, device_id=peer, device_id_type=MESH_ID)
    peers = len(peers_always)
    for present, peer in sides:
        @pl.when(present)
        def _():
            pl.semaphore_signal(barrier, 1, device_id=peer, device_id_type=MESH_ID)

        peers = peers + present.astype(jnp.int32)
    pl.semaphore_wait(barrier, peers)


def exchange_kernel(groups, own_ref, pos_ref, own_bins_ref, near_bins_ref, row_key_ref,
                    window_key_ref, grad_ref, partner_win, pos_win, own_rows, partial, held,
                    local_sem, sec_send, sec_recv, fwd_send, fwd_recv, halo_send, halo_recv,
                    part_sems):
    rows = own_ref.shape[0]
    piece = rows // PIECES
    sec, wide, grp, has_left, has_right, left_id, right_id = place_of(groups)
    partner_id = (1 - sec, wide, grp)
    me = wide * groups + grp
    left_cross = has_left & ((me - 1) // groups // Y_CHIPS != wide // Y_CHIPS)
    right_cross = has_right & ((me + 1) // groups // Y_CHIPS != wide // Y_CHIPS)
    cross = (left_cross, right_cross)
    across_id = tuple((1 - sec,) + tuple(peer[1:]) for peer in (left_id, right_id))

    pos_win[:, pl.ds(rows, rows)] = pos_ref[...]
    own_copy = pltpu.make_async_copy(own_ref, own_rows, local_sem.at[3])
    own_copy.start()
    win = 3 * rows
    empty = jnp.full((1, rows), -jnp.inf, jnp.float32)
    held[0, :, pl.ds(2 * rows, rows)] = empty
    held[1, :, pl.ds(0, rows)] = empty

    @pl.when(jnp.logical_not(has_left))
    def _():
        held[0, :, pl.ds(0, 2 * rows)] = jnp.full((1, 2 * rows), -jnp.inf, jnp.float32)

    @pl.when(jnp.logical_not(has_right))
    def _():
        held[1, :, pl.ds(rows, 2 * rows)] = jnp.full((1, 2 * rows), -jnp.inf, jnp.float32)

    for d, arrived in ((0, has_right), (1, has_left)):
        @pl.when(jnp.logical_not(arrived))
        def _():
            place = pl.ds((1 - d) * 2 * rows, rows)
            partner_win[place, :] = jnp.zeros((rows, partner_win.shape[1]), partner_win.dtype)
            pos_win[:, pl.ds((1 - d) * 2 * rows, rows)] = jnp.zeros(pos_ref.shape, jnp.int32)

    greet((partner_id,), ((has_left, left_id), (has_right, right_id),
                          (left_cross, across_id[0]), (right_cross, across_id[1])))

    def sec_copy(q):
        return pltpu.make_async_remote_copy(
            src_ref=own_ref.at[pl.ds(q * piece, piece)],
            dst_ref=partner_win.at[pl.ds(rows + q * piece, piece)],
            send_sem=sec_send.at[q], recv_sem=sec_recv.at[q],
            device_id=partner_id, device_id_type=MESH_ID)

    def pos_copy(d):
        return pltpu.make_async_remote_copy(
            src_ref=pos_ref,
            dst_ref=pos_win.at[:, pl.ds((1 - d) * 2 * rows, rows)],
            send_sem=halo_send.at[d], recv_sem=halo_recv.at[d],
            device_id=left_id if d == 0 else right_id, device_id_type=MESH_ID)

    def fwd_copy(d, q):
        return pltpu.make_async_remote_copy(
            src_ref=partner_win.at[pl.ds(rows + q * piece, piece)],
            dst_ref=partner_win.at[pl.ds((1 - d) * 2 * rows + q * piece, piece)],
            send_sem=fwd_send.at[d, q], recv_sem=fwd_recv.at[d, q],
            device_id=left_id if d == 0 else right_id, device_id_type=MESH_ID)

    def cross_copy(d, q):
        return pltpu.make_async_remote_copy(
            src_ref=own_ref.at[pl.ds(q * piece, piece)],
            dst_ref=partner_win.at[pl.ds((1 - d) * 2 * rows + q * piece, piece)],
            send_sem=fwd_send.at[d, q], recv_sem=fwd_recv.at[d, q],
            device_id=across_id[d], device_id_type=MESH_ID)

    sides = ((0, has_left), (1, has_right))
    for d, present in sides:
        @pl.when(present)
        def _():
            pos_copy(d).start()

        @pl.when(cross[d])
        def _():
            for q in range(PIECES):
                cross_copy(d, q).start()

    for q in range(IN_FLIGHT):
        sec_copy(q).start()
    for q in range(PIECES):
        sec_copy(q).wait_send()
        if q + IN_FLIGHT < PIECES:
            sec_copy(q + IN_FLIGHT).start()
        sec_copy(q).wait_recv()
        for d, present in sides:
            @pl.when(present & jnp.logical_not(cross[d]))
            def _():
                fwd_copy(d, q).start()

    own_copy.wait()
    own_block = own_rows[...]

    def block_scores(k):
        scores = logit_scale * lax.dot_general(
            own_block, partner_win[pl.ds(k * rows, rows), :], (((1,), (1,)), ((), ())),
            preferred_element_type=jnp.float32,
        )
        return scores, own_bins_ref[...] == near_bins_ref[:, pl.ds(k * rows, rows)]

    def block_totals(k):
        scores, allowed = block_scores(k)
        partial[:, pl.ds(k * rows, rows)] = masked_lse(scores, allowed, 0)
        return scores, allowed, masked_lse(scores, allowed, 1)

    centre = block_totals(1)

    for d, present in sides:
        arrived = has_right if d == 0 else has_left

        @pl.when(arrived)
        def _():
            pos_copy(d).wait_recv()
            for q in range(PIECES):
                fwd_copy(d, q).wait_recv()

    blocks = (block_totals(0), centre, block_totals(2))
    row_parts = [b[2] for b in blocks]
    top = jnp.maximum(jnp.maximum(row_parts[0], row_parts[1]), row_parts[2])
    top = jnp.where(top > -jnp.inf, top, 0.0)
    own_total = jnp.log(sum(jnp.exp(p - top) for p in row_parts)) + top

    def part_copy(d):
        return pltpu.make_async_remote_copy(
            src_ref=partial.at[:, pl.ds(d * rows, 2 * rows)],
            dst_ref=held.at[1 - d, :, pl.ds((1 - d) * rows, 2 * rows)],
            send_sem=part_sems.at[0, d], recv_sem=part_sems.at[1, d],
            device_id=left_id if d == 0 else right_id, device_id_type=MESH_ID)

    for d, present in sides:
        @pl.when(present)
        def _():
            part_copy(d).start()
    for d, present in sides:
        @pl.when(present)
        def _():
            part_copy(d).wait_send()

        arrived = has_right if d == 0 else has_left

        @pl.when(arrived)
        def _():
            part_copy(d).wait_recv()

    mine, left, right = partial[...], held[0], held[1]
    top = jnp.maximum(jnp.maximum(mine, left), right)
    top = jnp.where(top > -jnp.inf, top, 0.0)
    total = jnp.exp(mine - top) + jnp.exp(left - top) + jnp.exp(right - top)
    partner_total = jnp.log(total) + top

    col_key = jnp.where(sec == 0, window_key_ref[...], pos_win[...])
    grad = None
    for k, (scores, allowed, _) in enumerate(blocks):
        columns = slice(k * rows, (k + 1) * rows)
        hits = allowed & (row_key_ref[...] == col_key[:, columns])
        weights = jnp.exp(scores - own_total) + jnp.exp(scores - partner_total[:, columns])
        weights = jnp.where(allowed, weights, 0.0) - jnp.where(hits, 2.0, 0.0)
        term = jnp.dot(weights.astype(jnp.bfloat16), partner_win[pl.ds(k * rows, rows), :],
                       preferred_element_type=jnp.float32)
        grad = term if grad is None else grad + term
    grad_ref[...] = (logit_scale * grad).astype(grad_ref.dtype)

    for d, present in sides:
        @pl.when(present)
        def _():
            pos_copy(d).wait_send()

        @pl.when(present & jnp.logical_not(cross[d]))
        def _():
            for q in range(PIECES):
                fwd_copy(d, q).wait_send()

        @pl.when(cross[d])
        def _():
            for q in range(PIECES):
                cross_copy(d, q).wait_send()


def exchange(own, positives, own_bins, near_bins, row_key, window_key, groups):
    rows, features = own.shape
    anywhere = pl.BlockSpec(memory_space=pl.ANY)
    vmem = pl.BlockSpec(memory_space=pltpu.VMEM)
    return pl.pallas_call(
        functools.partial(exchange_kernel, groups),
        out_shape=jax.ShapeDtypeStruct((rows, features), own.dtype),
        in_specs=[anywhere] + [vmem] * 5,
        out_specs=vmem,
        scratch_shapes=[
            pltpu.VMEM((3 * rows, features), own.dtype),
            pltpu.VMEM((1, 3 * rows), jnp.int32),
            pltpu.VMEM((rows, features), own.dtype),
            pltpu.VMEM((1, 3 * rows), jnp.float32),
            pltpu.VMEM((2, 1, 3 * rows), jnp.float32),
            pltpu.SemaphoreType.DMA((4,)),
            pltpu.SemaphoreType.DMA((PIECES,)),
            pltpu.SemaphoreType.DMA((PIECES,)),
            pltpu.SemaphoreType.DMA((2, PIECES)),
            pltpu.SemaphoreType.DMA((2, PIECES)),
            pltpu.SemaphoreType.DMA((2,)),
            pltpu.SemaphoreType.DMA((2,)),
            pltpu.SemaphoreType.DMA((2, 2)),
        ],
        compiler_params=pltpu.CompilerParams(
            collective_id=0, has_side_effects=True, vmem_limit_bytes=48 * 1024 * 1024
        ),
    )(own, positives[None, :], own_bins, near_bins, row_key, window_key)


def masked_lse(scores, allowed, axis):
    top = jnp.max(jnp.where(allowed, scores, -jnp.inf), axis=axis, keepdims=True)
    top = jnp.where(top > -jnp.inf, top, 0.0)
    total = jnp.sum(jnp.where(allowed, jnp.exp(scores - top), 0.0), axis=axis, keepdims=True)
    return jnp.log(total) + top


def local(embeddings, bin_ids, positives):
    own = embeddings[0]
    row_count, features = own.shape
    blocks = row_count // BLOCK
    groups = lax.axis_size("grp")
    me = lax.axis_index(ROWS)
    first_row = me * row_count
    spectral = lax.axis_index("sec") == 0

    win = 3 * row_count

    padded = jnp.pad(bin_ids, blocks, constant_values=-1)
    near_bins = jnp.repeat(lax.dynamic_slice_in_dim(padded, me * blocks, 3 * blocks, 0), BLOCK)
    own_bins = jnp.repeat(lax.dynamic_slice_in_dim(bin_ids, me * blocks, blocks, 0), BLOCK)
    own_bins = own_bins[:, None]
    near_bins = near_bins[None, :]
    window_index = first_row - row_count + jnp.arange(win, dtype=jnp.int32)
    own_index = first_row + jnp.arange(row_count, dtype=jnp.int32)
    row_key = jnp.where(spectral, positives, own_index)[:, None]
    grad = exchange(own, positives, own_bins, near_bins, row_key, window_index[None, :], groups)
    return grad[None]


def solution(mesh):
    in_specs = (P("sec", ROWS, None), P(), P(ROWS))
    out_specs = P("sec", ROWS, None)
    return jax.shard_map(local, mesh=mesh, in_specs=in_specs, out_specs=out_specs, check_vma=False)
```

```python
import functools

import jax
import jax.numpy as jnp
from jax import lax
from jax.experimental import pallas as pl
from jax.experimental.pallas import tpu as pltpu
from jax.sharding import PartitionSpec as P

BLOCK = 256
logit_scale = 0.125
ROWS = ("wide", "grp")


MESH_ID = pl.DeviceIdType.MESH
PIECES = 8
IN_FLIGHT = 2
Y_CHIPS = 8


def place_of(groups):
    sec = lax.axis_index("sec")
    wide = lax.axis_index("wide")
    grp = lax.axis_index("grp")
    count = lax.axis_size("wide") * groups
    me = wide * groups + grp
    left = jnp.maximum(me - 1, 0)
    right = jnp.minimum(me + 1, count - 1)
    left_id = (sec, left // groups, left % groups)
    right_id = (sec, right // groups, right % groups)
    return sec, wide, grp, me > 0, me < count - 1, left_id, right_id


def greet(peers_always, sides):
    barrier = pltpu.get_barrier_semaphore()
    for peer in peers_always:
        pl.semaphore_signal(barrier, 1, device_id=peer, device_id_type=MESH_ID)
    peers = len(peers_always)
    for present, peer in sides:
        @pl.when(present)
        def _():
            pl.semaphore_signal(barrier, 1, device_id=peer, device_id_type=MESH_ID)

        peers = peers + present.astype(jnp.int32)
    pl.semaphore_wait(barrier, peers)


def exchange_kernel(groups, own_ref, pos_ref, own_bins_ref, near_bins_ref, row_key_ref,
                    window_key_ref, grad_ref, partner_win, pos_win, own_rows, partial, held,
                    local_sem, sec_send, sec_recv, fwd_send, fwd_recv, halo_send, halo_recv,
                    part_sems):
    rows = own_ref.shape[0]
    piece = rows // PIECES
    sec, wide, grp, has_left, has_right, left_id, right_id = place_of(groups)
    partner_id = (1 - sec, wide, grp)
    me = wide * groups + grp
    left_cross = has_left & ((me - 1) // groups // Y_CHIPS != wide // Y_CHIPS)
    right_cross = has_right & ((me + 1) // groups // Y_CHIPS != wide // Y_CHIPS)
    cross = (left_cross, right_cross)
    across_id = tuple((1 - sec,) + tuple(peer[1:]) for peer in (left_id, right_id))

    pos_win[:, pl.ds(rows, rows)] = pos_ref[...]
    own_copy = pltpu.make_async_copy(own_ref, own_rows, local_sem.at[3])
    own_copy.start()
    win = 3 * rows
    empty = jnp.full((1, rows), -jnp.inf, jnp.float32)
    held[0, :, pl.ds(2 * rows, rows)] = empty
    held[1, :, pl.ds(0, rows)] = empty

    @pl.when(jnp.logical_not(has_left))
    def _():
        held[0, :, pl.ds(0, 2 * rows)] = jnp.full((1, 2 * rows), -jnp.inf, jnp.float32)

    @pl.when(jnp.logical_not(has_right))
    def _():
        held[1, :, pl.ds(rows, 2 * rows)] = jnp.full((1, 2 * rows), -jnp.inf, jnp.float32)

    for d, arrived in ((0, has_right), (1, has_left)):
        @pl.when(jnp.logical_not(arrived))
        def _():
            place = pl.ds((1 - d) * 2 * rows, rows)
            partner_win[place, :] = jnp.zeros((rows, partner_win.shape[1]), partner_win.dtype)
            pos_win[:, pl.ds((1 - d) * 2 * rows, rows)] = jnp.zeros(pos_ref.shape, jnp.int32)

    greet((partner_id,), ((has_left, left_id), (has_right, right_id),
                          (left_cross, across_id[0]), (right_cross, across_id[1])))

    def sec_copy(q):
        return pltpu.make_async_remote_copy(
            src_ref=own_ref.at[pl.ds(q * piece, piece)],
            dst_ref=partner_win.at[pl.ds(rows + q * piece, piece)],
            send_sem=sec_send.at[q], recv_sem=sec_recv.at[q],
            device_id=partner_id, device_id_type=MESH_ID)

    def pos_copy(d):
        return pltpu.make_async_remote_copy(
            src_ref=pos_ref,
            dst_ref=pos_win.at[:, pl.ds((1 - d) * 2 * rows, rows)],
            send_sem=halo_send.at[d], recv_sem=halo_recv.at[d],
            device_id=left_id if d == 0 else right_id, device_id_type=MESH_ID)

    def fwd_copy(d, q):
        return pltpu.make_async_remote_copy(
            src_ref=partner_win.at[pl.ds(rows + q * piece, piece)],
            dst_ref=partner_win.at[pl.ds((1 - d) * 2 * rows + q * piece, piece)],
            send_sem=fwd_send.at[d, q], recv_sem=fwd_recv.at[d, q],
            device_id=left_id if d == 0 else right_id, device_id_type=MESH_ID)

    def cross_copy(d, q):
        return pltpu.make_async_remote_copy(
            src_ref=own_ref.at[pl.ds(q * piece, piece)],
            dst_ref=partner_win.at[pl.ds((1 - d) * 2 * rows + q * piece, piece)],
            send_sem=fwd_send.at[d, q], recv_sem=fwd_recv.at[d, q],
            device_id=across_id[d], device_id_type=MESH_ID)

    sides = ((0, has_left), (1, has_right))
    for d, present in sides:
        @pl.when(present)
        def _():
            pos_copy(d).start()

    for q in range(IN_FLIGHT):
        sec_copy(q).start()
    for q in range(PIECES):
        sec_copy(q).wait_send()
        if q + IN_FLIGHT < PIECES:
            sec_copy(q + IN_FLIGHT).start()
        sec_copy(q).wait_recv()
        for d, present in sides:
            @pl.when(present & jnp.logical_not(cross[d]))
            def _():
                fwd_copy(d, q).start()

    for d in range(2):
        @pl.when(cross[d])
        def _():
            for q in range(PIECES):
                cross_copy(d, q).start()

    own_copy.wait()
    own_block = own_rows[...]

    def block_scores(k):
        scores = logit_scale * lax.dot_general(
            own_block, partner_win[pl.ds(k * rows, rows), :], (((1,), (1,)), ((), ())),
            preferred_element_type=jnp.float32,
        )
        return scores, own_bins_ref[...] == near_bins_ref[:, pl.ds(k * rows, rows)]

    def block_totals(k):
        scores, allowed = block_scores(k)
        partial[:, pl.ds(k * rows, rows)] = masked_lse(scores, allowed, 0)
        return scores, allowed, masked_lse(scores, allowed, 1)

    centre = block_totals(1)

    for d, present in sides:
        @pl.when(present)
        def _():
            pos_copy(d).wait_send()

        @pl.when(present & jnp.logical_not(cross[d]))
        def _():
            for q in range(PIECES):
                fwd_copy(d, q).wait_send()

        @pl.when(cross[d])
        def _():
            for q in range(PIECES):
                cross_copy(d, q).wait_send()

        arrived = has_right if d == 0 else has_left

        @pl.when(arrived)
        def _():
            pos_copy(d).wait_recv()
            for q in range(PIECES):
                fwd_copy(d, q).wait_recv()

    blocks = (block_totals(0), centre, block_totals(2))
    row_parts = [b[2] for b in blocks]
    top = jnp.maximum(jnp.maximum(row_parts[0], row_parts[1]), row_parts[2])
    top = jnp.where(top > -jnp.inf, top, 0.0)
    own_total = jnp.log(sum(jnp.exp(p - top) for p in row_parts)) + top

    def part_copy(d):
        return pltpu.make_async_remote_copy(
            src_ref=partial.at[:, pl.ds(d * rows, 2 * rows)],
            dst_ref=held.at[1 - d, :, pl.ds((1 - d) * rows, 2 * rows)],
            send_sem=part_sems.at[0, d], recv_sem=part_sems.at[1, d],
            device_id=left_id if d == 0 else right_id, device_id_type=MESH_ID)

    for d, present in sides:
        @pl.when(present)
        def _():
            part_copy(d).start()
    for d, present in sides:
        @pl.when(present)
        def _():
            part_copy(d).wait_send()

        arrived = has_right if d == 0 else has_left

        @pl.when(arrived)
        def _():
            part_copy(d).wait_recv()

    mine, left, right = partial[...], held[0], held[1]
    top = jnp.maximum(jnp.maximum(mine, left), right)
    top = jnp.where(top > -jnp.inf, top, 0.0)
    total = jnp.exp(mine - top) + jnp.exp(left - top) + jnp.exp(right - top)
    partner_total = jnp.log(total) + top

    col_key = jnp.where(sec == 0, window_key_ref[...], pos_win[...])
    grad = None
    for k, (scores, allowed, _) in enumerate(blocks):
        columns = slice(k * rows, (k + 1) * rows)
        hits = allowed & (row_key_ref[...] == col_key[:, columns])
        weights = jnp.exp(scores - own_total) + jnp.exp(scores - partner_total[:, columns])
        weights = jnp.where(allowed, weights, 0.0) - jnp.where(hits, 2.0, 0.0)
        term = jnp.dot(weights.astype(jnp.bfloat16), partner_win[pl.ds(k * rows, rows), :],
                       preferred_element_type=jnp.float32)
        grad = term if grad is None else grad + term
    grad_ref[...] = (logit_scale * grad).astype(grad_ref.dtype)


def exchange(own, positives, own_bins, near_bins, row_key, window_key, groups):
    rows, features = own.shape
    anywhere = pl.BlockSpec(memory_space=pl.ANY)
    vmem = pl.BlockSpec(memory_space=pltpu.VMEM)
    return pl.pallas_call(
        functools.partial(exchange_kernel, groups),
        out_shape=jax.ShapeDtypeStruct((rows, features), own.dtype),
        in_specs=[anywhere] + [vmem] * 5,
        out_specs=vmem,
        scratch_shapes=[
            pltpu.VMEM((3 * rows, features), own.dtype),
            pltpu.VMEM((1, 3 * rows), jnp.int32),
            pltpu.VMEM((rows, features), own.dtype),
            pltpu.VMEM((1, 3 * rows), jnp.float32),
            pltpu.VMEM((2, 1, 3 * rows), jnp.float32),
            pltpu.SemaphoreType.DMA((4,)),
            pltpu.SemaphoreType.DMA((PIECES,)),
            pltpu.SemaphoreType.DMA((PIECES,)),
            pltpu.SemaphoreType.DMA((2, PIECES)),
            pltpu.SemaphoreType.DMA((2, PIECES)),
            pltpu.SemaphoreType.DMA((2,)),
            pltpu.SemaphoreType.DMA((2,)),
            pltpu.SemaphoreType.DMA((2, 2)),
        ],
        compiler_params=pltpu.CompilerParams(
            collective_id=0, has_side_effects=True, vmem_limit_bytes=48 * 1024 * 1024
        ),
    )(own, positives[None, :], own_bins, near_bins, row_key, window_key)


def masked_lse(scores, allowed, axis):
    top = jnp.max(jnp.where(allowed, scores, -jnp.inf), axis=axis, keepdims=True)
    top = jnp.where(top > -jnp.inf, top, 0.0)
    total = jnp.sum(jnp.where(allowed, jnp.exp(scores - top), 0.0), axis=axis, keepdims=True)
    return jnp.log(total) + top


def local(embeddings, bin_ids, positives):
    own = embeddings[0]
    row_count, features = own.shape
    blocks = row_count // BLOCK
    groups = lax.axis_size("grp")
    me = lax.axis_index(ROWS)
    first_row = me * row_count
    spectral = lax.axis_index("sec") == 0

    win = 3 * row_count

    padded = jnp.pad(bin_ids, blocks, constant_values=-1)
    near_bins = jnp.repeat(lax.dynamic_slice_in_dim(padded, me * blocks, 3 * blocks, 0), BLOCK)
    own_bins = jnp.repeat(lax.dynamic_slice_in_dim(bin_ids, me * blocks, blocks, 0), BLOCK)
    own_bins = own_bins[:, None]
    near_bins = near_bins[None, :]
    window_index = first_row - row_count + jnp.arange(win, dtype=jnp.int32)
    own_index = first_row + jnp.arange(row_count, dtype=jnp.int32)
    row_key = jnp.where(spectral, positives, own_index)[:, None]
    grad = exchange(own, positives, own_bins, near_bins, row_key, window_index[None, :], groups)
    return grad[None]


def solution(mesh):
    in_specs = (P("sec", ROWS, None), P(), P(ROWS))
    out_specs = P("sec", ROWS, None)
    return jax.shard_map(local, mesh=mesh, in_specs=in_specs, out_specs=out_specs, check_vma=False)
```
